128 devices in a mesh: gx: 8 (over x, core), gy: 16 (over y, z).
Axes of the slice: x: 4, y: 4, z: 4, core: 2. Of those that a mesh axis runs over, the one named last changes fastest.
Arguments:
- adjoint_state: float32 [4, 50, 128, 2048], P(None, None, 'gx', 'gy'), may hold values from -6 to 6
- velocity: float32 [2, 50, 128, 2048], P(None, None, 'gx', 'gy'), may hold values from -1.5 to 1.5
- diffusivity: float32 [128, 2048], P('gx', 'gy'), may hold values from 0.02 to 0.2
- mixing: float32 [128, 2048], P('gx', 'gy'), may hold values from 0.1 to 10
- wet_levels: int32 [128, 2048], P('gx', 'gy'), may hold values from 0 to 50
- innovations: float32 [262144, 128], P(('gx', 'gy')), may hold values from -6 to 6
- owner_tile: int32 [262144, 1], P(('gx', 'gy')), may hold values from 0 to 127; in each aligned block of 2048 rows (0 to 2047, 2048 to 4095, ...) at most 24 rows name the same one
- cell_index: int32 [262144], P(('gx', 'gy')), may hold values from 0 to 1904
- offsets: float32 [2, 262144], P(None, ('gx', 'gy')), may hold values from 0 to 1
- live_counts: int32 [128], P(('gx', 'gy')), may hold values from 1 to 2048, 196608 in all
- depth_weights: float32 [64, 50], replicated, may hold values from -0.75 to 0.75
Outputs:
- adjoint_result: float32 [4, 50, 128, 2048], P(None, None, 'gx', 'gy')
The draws below stay inside these ranges and needn't reach their ends.
Inputs may be any that keep to these rules, and one draw needn't show every extreme that they name: owner_tile[o, 0] is the index gx * 16 + gy of the tile that holds observation o; among the 2048 rows of one device, in use or not, no tile is named more than 24 times. cell_index[o] = i * 127 + j names local cell (i, j) of the owning tile, so that all four corner cells lie in that tile. The first live_counts[s] rows of device s are in use.
All inputs are finite; a program needn't handle non-finite values.
Results may differ from the reference program's by a relative error of at most 0.0001.
Values sent between devices are 32-bit elements; how exact they have to be, the bound alone decides.
A program may use at most 128 MiB of HBM per device.

```python
import math
import jax
import jax.numpy as jnp
import numpy as np
from jax import lax

LEV = 50
PROF = 64
OBSW = 128
CX = 16
CY = 128
OBS_DEV = 2048
NX = 128
NY = 2048
OBS = 262144
CAP = 24
N_GY = 16
DEVICES = 128


def touch_ends(entries, stream_key, low, top_value):
    place = [jax.random.randint(jax.random.fold_in(stream_key, axis), (), 0, length) for axis, length in enumerate(entries.shape)]
    widest = entries.shape.index(max(entries.shape))
    neighbour = place[:widest] + [(place[widest] + 1) % entries.shape[widest]] + place[widest + 1:]
    return entries.at[tuple(place)].set(low).at[tuple(neighbour)].set(top_value)


def shard_levels(stream_key, shape, shards, smallest, largest):
    loudness = 1.0
    for position, parts in shards:
        heights = jax.random.uniform(jax.random.fold_in(jax.random.fold_in(stream_key, 6), position), (parts,), jnp.float32, smallest / len(shards), largest / len(shards))
        loudness = loudness * jnp.repeat(jnp.exp(heights), shape[position] // parts).reshape((-1,) + (1,) * (len(shape) - 1 - position))
    return loudness


def length_profile(number_of, total, limit, lean):
    loads = [(1 << 20) // math.isqrt(rank ** lean) + 1 for rank in range(2, number_of + 1)]
    rest, counts = total - limit - (number_of - 1), [1] * (number_of - 1)
    while rest > 0:
        free = [i for i in range(number_of - 1) if counts[i] < limit]
        pool, left = sum([loads[i] for i in free]), rest
        for i in free:
            more = min(limit - counts[i], max(1, left * loads[i] // pool), rest)
            counts[i] = counts[i] + more
            rest = rest - more
    return np.array([limit] + counts)


def uneven_parts(key, number_of, total, reach, slope):
    if number_of == 2:
        one = jax.random.randint(key, (), max(1, total - reach), min(reach, total - 1) + 1)
        return jnp.stack([one, total - one])
    tallies = jnp.asarray(length_profile(number_of, total, reach, slope), jnp.int32)
    pairs = (number_of - 1) // 2
    giver, receiver = tallies[1:1 + 2 * pairs:2], tallies[2:2 + 2 * pairs:2]
    margin = jnp.minimum(giver - 1, reach - receiver)
    moved = jax.random.randint(jax.random.fold_in(key, 1), (pairs,), 0, 1 << 20) % (margin + 1)
    tallies = tallies.at[1:1 + 2 * pairs:2].set(giver - moved).at[2:2 + 2 * pairs:2].set(receiver + moved)
    return tallies[jax.random.permutation(jax.random.fold_in(key, 2), number_of)]


def shared_out(stream_key, own, number, rows, number_of, top, limit, slope):
    ranking = jax.random.permutation(stream_key, number_of)
    heavy_load, usual = load_shares(number_of, rows * top, limit, slope, True), load_shares(number_of, rows * top, limit, slope, False)
    places = jnp.arange(number_of)

    def named(sizes, turn):
        used = int((sizes > 0).sum())
        fixed = max(1, used // 4)
        passed = fixed + (places - fixed + turn * (used - fixed)) % max(1, number_of - fixed)
        return jnp.zeros((number_of,), jnp.int32).at[ranking[jnp.where(places < fixed, places, passed)]].set(jnp.asarray(sizes, jnp.int32))

    sizes = jnp.where(number % 4 == 0, named(heavy_load, number // 4), named(usual, number - number // 4 - 1))
    mixed = jax.random.permutation(jax.random.fold_in(own, 3), number_of)
    donor, sink = mixed[0:number_of // 2 * 2:2], mixed[1:number_of // 2 * 2:2]
    room = jnp.minimum(sizes[donor] - 1, limit - sizes[sink]) // 2
    room = jnp.where((donor == ranking[0]) | (sink == ranking[0]) | (sizes[sink] == 0), 0, jnp.maximum(room, 0))
    passed = jax.random.randint(jax.random.fold_in(own, 4), (number_of // 2,), 0, 1 << 20) % (room + 1)
    sizes = sizes.at[donor].add(-passed).at[sink].add(passed)
    labels = jnp.searchsorted(jnp.cumsum(sizes), jnp.arange(rows * top), side="right").astype(jnp.int32)
    table = labels.reshape(top, rows).T
    table = table[jax.random.permutation(jax.random.fold_in(own, 1), rows)]
    turn = jax.random.randint(jax.random.fold_in(own, 2), (rows, 1), 0, top)
    return jnp.take_along_axis(table, (jnp.arange(top)[None, :] + turn) % top, axis=1)


def load_shares(number_of, total, reach, lean, full):
    loads = [(1 << 20) // math.isqrt(standing ** lean) + 1 for standing in range(1, number_of + 1)]
    largest = reach if full else min(reach, max(-(-total // number_of), total * loads[0] // sum(loads)))
    least = 1 if total - largest >= number_of - 1 else 0
    holding, spare = [largest] + [least] * (number_of - 1), total - largest - least * (number_of - 1)
    while spare > 0:
        movable = [i for i in range(1, number_of) if holding[i] < largest] or [i for i in range(1, number_of) if holding[i] < reach]
        whole, left = sum([loads[i] for i in movable]), spare
        for i in movable:
            more = min(reach - holding[i], max(1, left * loads[i] // whole), spare)
            holding[i] = holding[i] + more
            spare = spare - more
    return np.array(holding)


def noise(rng, dims, scale, reach, cuts=(), dtype=jnp.bfloat16):
    factor_of = shard_levels(rng, dims, cuts, -0.22, 0.18) if cuts else 1.0
    array = jax.random.normal(rng, dims, jnp.float32) * scale * factor_of
    return jnp.minimum(jnp.maximum(array, -reach), reach).astype(dtype)


def setup_inputs(seed: int = 0) -> dict:
    arg_keys = jax.random.split(jax.random.key(seed), 12)
    adjoint_state = noise(arg_keys[0], (4, LEV, NX, NY), 1.0, 6.0, ((2, 8), (3, 16)), jnp.float32)
    velocity = noise(arg_keys[1], (2, LEV, NX, NY), 0.3, 1.5, ((2, 8), (3, 16)), jnp.float32)
    diffusivity = jnp.clip(jnp.exp(math.log(0.2) - 2.3025851 * jax.random.uniform(arg_keys[2], (NX, NY), jnp.float32) ** shard_levels(arg_keys[2], (NX, NY), ((0, 8), (1, 16)), -0.2, 0.2)), 0.02, 0.2)
    mixing = jnp.clip(jnp.exp(math.log(10.0) - 4.6051702 * jax.random.uniform(arg_keys[3], (NX, NY), jnp.float32) ** shard_levels(arg_keys[3], (NX, NY), ((0, 8), (1, 16)), -0.2, 0.2)), 0.1, 10.0)
    wet_levels = touch_ends(jax.random.randint(arg_keys[4], (NX, NY), 0, LEV + 1), jax.random.fold_in(arg_keys[4], 1), 0, LEV).astype(jnp.int32)
    innovations = noise(arg_keys[5], (OBS, OBSW), 1.0, 6.0, ((0, 128),), jnp.float32)
    owner_tile_keys = jax.random.split(jax.random.fold_in(arg_keys[6], 1), OBS // OBS_DEV)
    owner_tile_turns = jax.random.permutation(jax.random.fold_in(arg_keys[6], 3), OBS // OBS_DEV)
    owner_tile = jax.vmap(lambda own, number: shared_out(jax.random.fold_in(arg_keys[6], 2), own, number, OBS_DEV, DEVICES, 1, CAP, 2))(owner_tile_keys, owner_tile_turns).reshape((OBS, 1))
    cell_index = touch_ends(jax.random.randint(arg_keys[7], (OBS,), 0, (CX - 1) * (CY - 1)), jax.random.fold_in(arg_keys[7], 1), 0, ((CX - 1) * (CY - 1)) - 1).astype(jnp.int32)
    offsets = jnp.clip(1.0 * jax.random.uniform(arg_keys[8], (2, OBS), jnp.float32) ** shard_levels(arg_keys[8], (2, OBS), ((1, 128),), -0.2, 0.2), 0.0, 1.0)
    live_counts = uneven_parts(arg_keys[9], DEVICES, 3 * OBS_DEV * DEVICES // 4, OBS_DEV, 1).astype(jnp.int32)
    depth_weights = noise(arg_keys[10], (PROF, LEV), PROF ** -0.5, 0.75, (), jnp.float32)
    return {"adjoint_state": adjoint_state, "velocity": velocity, "diffusivity": diffusivity, "mixing": mixing, "wet_levels": wet_levels, "innovations": innovations, "owner_tile": owner_tile, "cell_index": cell_index, "offsets": offsets, "live_counts": live_counts, "depth_weights": depth_weights}


pressure_heat = 0.2
pressure_salt = 0.15
coriolis_peak = 0.2


def wet_mask(wet_levels, levels):
    depth_rank = lax.broadcasted_iota(jnp.int32, (levels,) + wet_levels.shape, 0)
    return (depth_rank < wet_levels[None]).astype(jnp.float32)


def column_solve(field, mixing):
    levels = field.shape[1]
    edge_diag = 1.0 + mixing
    inner_diag = 1.0 + 2.0 * mixing
    upper_now = -mixing / edge_diag
    value_now = field[:, 0] / edge_diag
    uppers = [upper_now]
    values = [value_now]
    for depth_level in range(1, levels):
        diag_now = edge_diag if depth_level == levels - 1 else inner_diag
        pivot_now = diag_now + mixing * upper_now
        value_now = (field[:, depth_level] + mixing * value_now) / pivot_now
        upper_now = -mixing / pivot_now
        uppers.append(upper_now)
        values.append(value_now)
    below_now = values[-1]
    result = [below_now]
    for depth_level in range(levels - 2, -1, -1):
        below_now = values[depth_level] - uppers[depth_level] * below_now
        result.append(below_now)
    return jnp.stack(result[::-1], axis=1)


def diff_east(field):
    return (8.0 * (field[..., 3:-1, :] - field[..., 1:-3, :]) - (field[..., 4:, :] - field[..., :-4, :])) / 12.0


def diff_north(field):
    return (8.0 * (field[..., 3:-1] - field[..., 1:-3]) - (field[..., 4:] - field[..., :-4])) / 12.0


def explicit(extended, velocity, diffusivity, coriolis):
    flux_east = velocity[0] * extended
    flux_north = velocity[1] * extended
    carried = diff_east(flux_east[..., 2:-2]) + diff_north(flux_north[..., 2:-2, :])
    spread = diffusivity * extended
    diffused = (spread[..., 3:-1, 2:-2] + spread[..., 1:-3, 2:-2] + spread[..., 2:-2, 3:-1]
                + spread[..., 2:-2, 1:-3] - 4.0 * spread[..., 2:-2, 2:-2])
    centre = extended[..., 2:-2, 2:-2]
    pressure = diff_east(extended[2][..., 2:-2]) + diff_north(extended[3][..., 2:-2, :])
    summed = centre + carried + diffused
    return jnp.stack([summed[0] + pressure_heat * pressure,
                      summed[1] - pressure_salt * pressure,
                      summed[2] - coriolis * centre[3],
                      summed[3] + coriolis * centre[2]], axis=0)


def coriolis_rows(row_count, total_rows, first_row):
    row_place = lax.broadcasted_iota(jnp.int32, (row_count,), 0) + first_row
    return coriolis_peak * (2.0 * (row_place.astype(jnp.float32) + 0.5) / total_rows - 1.0)


def forcing_field(innovations, owner_tile, cell_index, offsets, live_counts, depth_weights):
    obs_count = innovations.shape[0]
    row_index = lax.broadcasted_iota(jnp.int32, (obs_count,), 0)
    source_dev = row_index // OBS_DEV
    live_flag = (row_index - source_dev * OBS_DEV < live_counts[source_dev]).astype(jnp.float32)
    kept_rows = innovations * live_flag[:, None]
    profile = jnp.dot(kept_rows.reshape(obs_count * 2, PROF), depth_weights,
                      precision=lax.Precision.HIGHEST,
                      preferred_element_type=jnp.float32).reshape(obs_count, 2, LEV)
    values = profile.transpose(1, 2, 0)
    tile_index = owner_tile[:, 0]
    grid_row = (tile_index // N_GY) * CX + cell_index // (CY - 1)
    grid_col = (tile_index % N_GY) * CY + cell_index % (CY - 1)
    offset_one = offsets[0]
    offset_two = offsets[1]
    forcing = jnp.zeros((2, LEV, NX, NY), jnp.float32)
    corners = ((0, 0, (1.0 - offset_one) * (1.0 - offset_two)),
               (1, 0, offset_one * (1.0 - offset_two)),
               (0, 1, (1.0 - offset_one) * offset_two),
               (1, 1, offset_one * offset_two))
    for step_row, step_col, weight in corners:
        forcing = forcing.at[:, :, grid_row + step_row, grid_col + step_col].add(weight * values)
    return forcing


def reference(adjoint_state, velocity, diffusivity, mixing, wet_levels, innovations, owner_tile, cell_index, offsets, live_counts, depth_weights):
    forcing = forcing_field(innovations, owner_tile, cell_index, offsets, live_counts, depth_weights)
    adjoint_now = adjoint_state + jnp.concatenate([forcing, jnp.zeros_like(forcing)], axis=0)
    wet_share = wet_mask(wet_levels, LEV)
    coriolis = coriolis_rows(NY, NY, 0)
    velocity_pad = jnp.pad(velocity, ((0, 0), (0, 0), (2, 2), (2, 2)))
    diffusion_pad = jnp.pad(diffusivity, 2)

    def explicit_level(pieces):
        return explicit(pieces[0], pieces[1], diffusion_pad, coriolis)

    for repeat in range(2):
        solved = column_solve(adjoint_now * wet_share, mixing)
        padded = jnp.pad(solved, ((0, 0), (0, 0), (2, 2), (2, 2)))
        adjoint_now = lax.map(explicit_level, (padded.transpose(1, 0, 2, 3),
                                               velocity_pad.transpose(1, 0, 2, 3))).transpose(1, 0, 2, 3)
    return adjoint_now * wet_share
```

```python
import functools

import jax
import jax.numpy as jnp
from jax import lax
from jax.experimental import pallas as pl
from jax.experimental.pallas import tpu as pltpu
from jax.sharding import PartitionSpec as P

F32 = jnp.float32
BF16 = jnp.bfloat16
MESH = pl.DeviceIdType.MESH

PRESSURE_HEAT = 0.2
PRESSURE_SALT = 0.15
CORIOLIS_PEAK = 0.2

CAP = 24
LANES = 128
SUB = 8
PAD = 4


def split(value):
    high = value.astype(BF16)
    return high, (value - high.astype(F32)).astype(BF16)


def pack_kernel(
    live_ref, target_ref, cell_ref, offset_ref, rows_ref, weights_ref, send_ref, packed, slots, *, tiles, levels, deep
):
    obs = rows_ref.shape[0]
    prof = weights_ref.shape[0]
    block = send_ref.shape[0]
    step = pl.program_id(0)

    @pl.when(step == 0)
    def _():
        wide = jnp.concatenate([weights_ref[...], jnp.zeros((prof, LANES - levels), F32)], axis=1)
        both = jnp.concatenate([wide, pltpu.roll(wide, deep, 1)], axis=0)
        tri = (
            lax.broadcasted_iota(jnp.int32, (256, 256), 0) < lax.broadcasted_iota(jnp.int32, (256, 256), 1)
        ).astype(BF16)
        tile_place = lax.broadcasted_iota(jnp.int32, (tiles, 256), 0)
        carry = jnp.zeros((tiles, 1), F32)
        for part in range(obs // 256):
            span = slice(part * 256, (part + 1) * 256)
            place = lax.broadcasted_iota(jnp.int32, (1, 256), 1) + part * 256
            live = place < live_ref[0]
            target = target_ref[:, span]
            named = ((tile_place == target) & live).astype(F32)
            before = jnp.dot(named.astype(BF16), tri, preferred_element_type=F32) + carry
            rank = jnp.sum(named * before, axis=0, keepdims=True)
            carry = carry + jnp.sum(named, axis=1, keepdims=True)
            slots[:, span] = jnp.where(live, target * CAP + rank.astype(jnp.int32), -1)
            cell = cell_ref[:, span].astype(F32)
            row = jnp.floor((cell + 0.5) * (1.0 / 127.0))
            col = cell - 127.0 * row
            for half in range(2):
                cut = slice(half * LANES, (half + 1) * LANES)
                here = slice(part * 256 + half * LANES, part * 256 + (half + 1) * LANES)
                side = jnp.concatenate(
                    [
                        jnp.zeros((2 * deep, LANES), F32),
                        row[:, cut],
                        col[:, cut],
                        offset_ref[:, here],
                        jnp.zeros((LANES - 2 * deep - 4, LANES), F32),
                    ],
                    axis=0,
                )
                profile = jnp.dot(rows_ref[here, :], both, precision=lax.Precision.HIGHEST, preferred_element_type=F32)
                high, low = split(profile + side.T)
                packed[here, :LANES] = high
                packed[here, LANES:] = low

    slot_place = lax.broadcasted_iota(jnp.int32, (block, 1), 0) + step * block
    pick = (slot_place == slots[...]).astype(F32).astype(BF16)
    got = jnp.dot(pick, packed[...], preferred_element_type=F32)
    send_ref[...] = got[:, :LANES] + got[:, LANES:]


def pack(innovations, target, cell, offsets, live, weights, tiles, levels, deep):
    obs = innovations.shape[0]
    slots = tiles * CAP
    block = 256
    whole = lambda shape: pl.BlockSpec(shape, lambda i: (0,) * len(shape))
    return pl.pallas_call(
        functools.partial(pack_kernel, tiles=tiles, levels=levels, deep=deep),
        grid=(slots // block,),
        in_specs=[
            pl.BlockSpec(memory_space=pltpu.SMEM),
            whole((1, obs)),
            whole((1, obs)),
            whole((2, obs)),
            whole((obs, LANES)),
            whole(weights.shape),
        ],
        out_specs=pl.BlockSpec((block, LANES), lambda i: (i, 0)),
        out_shape=jax.ShapeDtypeStruct((slots, LANES), F32),
        scratch_shapes=[pltpu.VMEM((obs, 2 * LANES), BF16), pltpu.VMEM((1, obs), jnp.int32)],
        compiler_params=pltpu.CompilerParams(vmem_limit_bytes=48 << 20),
        name="pack_rows",
    )(live, target, cell, offsets, innovations, weights)


def scatter_kernel(rows_ref, forcing_ref, values, sides, columns, *, deep):
    count = rows_ref.shape[0]
    x = pl.program_id(0)

    @pl.when(x == 0)
    def _():
        lane = lax.broadcasted_iota(jnp.int32, (LANES, LANES), 1)
        y_place = lax.broadcasted_iota(jnp.int32, (LANES, LANES), 0).astype(F32)

        @pl.loop(0, count // LANES)
        def _(part):
            here = pl.ds(pl.multiple_of(part * LANES, LANES), LANES)
            block = rows_ref[here, :]
            high, low = split(jnp.where(lane < 2 * deep, block, 0.0))
            values[here, :LANES] = high
            values[here, LANES:] = low
            side = block.T[2 * deep : 2 * deep + SUB, :]
            sides[:, here] = side
            col, north = side[1:2, :], side[3:4, :]
            columns[:, here] = jnp.where(y_place == col, 1.0 - north, 0.0) + jnp.where(y_place == col + 1.0, north, 0.0)

    row, east = sides[0:1, :], sides[2:3, :]
    x_now = x.astype(F32)
    share = jnp.where(row == x_now, 1.0 - east, 0.0) + jnp.where(row + 1.0 == x_now, east, 0.0)
    high, low = split(columns[...] * share)
    got = jnp.dot(jnp.concatenate([high, low], axis=0), values[...], preferred_element_type=F32)
    plane = got[:LANES, :LANES] + got[:LANES, LANES:] + got[LANES:, :LANES]
    forcing_ref[0] = plane.T[: 2 * deep, :]


def scatter(rows, tile_rows, deep):
    count = rows.shape[0]
    return pl.pallas_call(
        functools.partial(scatter_kernel, deep=deep),
        grid=(tile_rows,),
        in_specs=[pl.BlockSpec((count, LANES), lambda i: (0, 0))],
        out_specs=pl.BlockSpec((1, 2 * deep, LANES), lambda i: (i, 0, 0)),
        out_shape=jax.ShapeDtypeStruct((tile_rows, 2 * deep, LANES), F32),
        scratch_shapes=[
            pltpu.VMEM((count, 2 * LANES), BF16),
            pltpu.VMEM((SUB, count), F32),
            pltpu.VMEM((LANES, count), F32),
        ],
        compiler_params=pltpu.CompilerParams(vmem_limit_bytes=48 << 20),
        name="scatter_rows",
    )(rows)


def steps_kernel(
    state_ref, forcing_ref, velocity_ref, diffusion_ref, mixing_ref, wet_ref, out_ref,
    field, east, north_a, north_b, north_m, north_p, kappa, result, inverse, gain, going,
    edge_lo, edge_hi, x_send, x_recv, y_send, y_recv, send_sem, recv_sem,
    *, levels, deep, span_x, span_y, total_rows,
):
    tile_x, tile_y = mixing_ref.shape
    rows = tile_x * deep
    wide = tile_x + 2 * PAD
    me_x, me_y = lax.axis_index("gx"), lax.axis_index("gy")
    west, right = lax.rem(me_x + span_x - 1, span_x), lax.rem(me_x + 1, span_x)
    south, up = lax.rem(me_y + span_y - 1, span_y), lax.rem(me_y + 1, span_y)
    peers = ((west, me_y), (right, me_y), (me_x, south), (me_x, up))

    barrier = pltpu.get_barrier_semaphore()
    for peer in peers:
        pl.semaphore_signal(barrier, inc=1, device_id=peer, device_id_type=MESH)

    mixing = mixing_ref[...]
    lane = lax.broadcasted_iota(jnp.int32, (1, tile_y), 1)
    third, twelfth = 8.0 / 12.0, 1.0 / 12.0

    def coefficient(l, q_before):
        diag = 1.0 + mixing * jnp.where((l == 0) | (l == levels - 1), 1.0, 2.0)
        q = 1.0 / (diag - mixing * mixing * q_before)
        inverse[l] = q
        gain[l] = mixing * q
        return q

    lax.fori_loop(0, levels, coefficient, jnp.zeros_like(mixing))

    zero_rows = jnp.zeros((PAD * deep, tile_y), F32)
    for c in range(4):
        field[c, : PAD * deep, :] = zero_rows
        field[c, (PAD + tile_x) * deep :, :] = zero_rows
    east[: PAD * deep, :] = zero_rows
    east[(PAD + tile_x) * deep :, :] = zero_rows
    kappa[...] = jnp.zeros_like(kappa)
    kappa[PAD : PAD + tile_x, :] = diffusion_ref[...]

    @pl.loop(0, deep - levels)
    def _(extra):
        blank = jnp.zeros((tile_x, tile_y), F32)
        for c in range(4):
            field[c, pl.ds(PAD * deep + levels + extra, tile_x, stride=deep), :] = blank
            result[c, pl.ds(levels + extra, tile_x, stride=deep), :] = blank
        east[pl.ds(PAD * deep + levels + extra, tile_x, stride=deep), :] = blank
        for table in (north_a, north_b, north_m, north_p):
            table[pl.ds(levels + extra, tile_x, stride=deep), :] = blank

    diffusion = diffusion_ref[...]
    mask_a = (lane >= 1).astype(F32)
    mask_b = (lane < tile_y - 1).astype(F32)
    mask_m = (lane >= 2).astype(F32)
    mask_p = (lane < tile_y - 2).astype(F32)

    @pl.loop(0, levels)
    def _(l):
        u, v = velocity_ref[0, l], velocity_ref[1, l]
        east[pl.ds(PAD * deep + l, tile_x, stride=deep), :] = u
        here = pl.ds(l, tile_x, stride=deep)
        north_a[here, :] = (third * v + diffusion) * mask_a
        north_b[here, :] = (diffusion - third * v) * mask_b
        north_m[here, :] = (twelfth * v) * mask_m
        north_p[here, :] = (twelfth * v) * mask_p

    @pl.loop(0, rows // LANES)
    def _(part):
        here = pl.ds(pl.multiple_of(part * LANES, LANES), LANES)
        edge_lo[0, :, here] = north_b[here, :].T[:SUB, :]
        edge_lo[1, :, here] = north_p[here, :].T[:SUB, :]
        edge_hi[0, :, here] = north_a[here, :].T[tile_y - SUB :, :]
        edge_hi[1, :, here] = north_m[here, :].T[tile_y - SUB :, :]

    cor = CORIOLIS_PEAK * (2.0 * ((lane + me_y * tile_y).astype(F32) + 0.5) / total_rows - 1.0)
    wet = wet_ref[...]
    pressure = (PRESSURE_HEAT, -PRESSURE_SALT)

    def x_part(c, x, t, push):
        def at(shift):
            return pl.ds(pl.multiple_of((x + shift) * deep, SUB) + t * SUB, SUB)

        def coef(shift):
            return third * east[at(shift), :], kappa[pl.ds(x + shift, 1), :]

        (flow_up, kap_up), (flow_down, kap_down) = coef(1), coef(-1)
        total = (
            (flow_up + kap_up) * field[c, at(1), :]
            + (kap_down - flow_down) * field[c, at(-1), :]
            - twelfth * (east[at(2), :] * field[c, at(2), :] - east[at(-2), :] * field[c, at(-2), :])
        )
        return total if push is None else total + pressure[c] * push

    def x_push(x, t):
        def at(shift):
            return pl.ds(pl.multiple_of((x + shift) * deep, SUB) + t * SUB, SUB)

        return third * (field[2, at(1), :] - field[2, at(-1), :]) - twelfth * (field[2, at(2), :] - field[2, at(-2), :])

    pl.semaphore_wait(barrier, 4)

    for turn in range(2):
        def down(l, before):
            now = []
            q, p = inverse[l], gain[l]
            under = l < wet
            for c in range(4):
                if turn == 0:
                    value = state_ref[c, l]
                    if c < 2:
                        value = value + forcing_ref[pl.ds(c * deep + l, tile_x, stride=2 * deep), :]
                else:
                    value = result[c, pl.ds(l, tile_x, stride=deep), :]
                value = jnp.where(under, value, 0.0) * q + p * before[c]
                going[c, l] = value
                now.append(value)
            return tuple(now)

        lax.fori_loop(0, levels, down, (jnp.zeros((tile_x, tile_y), F32),) * 4)

        def rise(k, below):
            l = levels - 1 - k
            p = jnp.where(k == 0, 0.0, 1.0) * gain[l]
            now = []
            for c in range(4):
                value = going[c, l] + p * below[c]
                field[c, pl.ds(PAD * deep + l, tile_x, stride=deep), :] = value
                now.append(value)
            return tuple(now)

        lax.fori_loop(0, levels, rise, (jnp.zeros((tile_x, tile_y), F32),) * 4)

        copies = []
        for side in range(2):
            for place in range(2):
                x = (PAD - 2 + place) if side == 0 else (PAD + tile_x + place)
                for t in range(deep // SUB):
                    push = x_push(x, t)
                    for c in range(4):
                        x_send[turn, side, place, c, t * SUB : (t + 1) * SUB, :] = x_part(c, x, t, push if c < 2 else None)
            copy = pltpu.make_async_remote_copy(
                src_ref=x_send.at[turn, side],
                dst_ref=x_recv.at[turn, side],
                send_sem=send_sem.at[turn, side],
                recv_sem=recv_sem.at[turn, side],
                device_id=peers[side],
                device_id_type=MESH,
            )
            copy.start()
            copies.append(copy)

        @pl.loop(0, rows // LANES)
        def _(part):
            here = pl.ds(pl.multiple_of(part * LANES, LANES), LANES)
            there = pl.ds(pl.multiple_of(part * LANES + PAD * deep, SUB), LANES)
            turned = [field[c, there, :].T for c in range(4)]
            b_lo, c_lo = edge_lo[0, :, here], edge_lo[1, :, here]
            a_hi, c_hi = edge_hi[0, :, here], edge_hi[1, :, here]
            a_lo, b_hi = b_lo + 16.0 * c_lo, a_hi - 16.0 * c_hi
            e_lo = [value[:SUB, :] for value in turned]
            e_hi = [value[tile_y - SUB :, :] for value in turned]
            for c in range(4):
                flow_a, flow_c = a_lo * e_lo[c], c_lo * e_lo[c]
                flow_b, flow_d = b_hi * e_hi[c], c_hi * e_hi[c]
                if c < 2:
                    flow_a = flow_a + pressure[c] * third * e_lo[3]
                    flow_c = flow_c + pressure[c] * twelfth * e_lo[3]
                    flow_b = flow_b - pressure[c] * third * e_hi[3]
                    flow_d = flow_d + pressure[c] * twelfth * e_hi[3]
                y_send[turn, 0, 2 * c : 2 * c + 1, here] = -flow_c[0:1, :]
                y_send[turn, 0, 2 * c + 1 : 2 * c + 2, here] = flow_a[0:1, :] - flow_c[1:2, :]
                y_send[turn, 1, 2 * c : 2 * c + 1, here] = flow_b[7:8, :] + flow_d[6:7, :]
                y_send[turn, 1, 2 * c + 1 : 2 * c + 2, here] = flow_d[7:8, :]

        for side in range(2):
            copy = pltpu.make_async_remote_copy(
                src_ref=y_send.at[turn, side],
                dst_ref=y_recv.at[turn, side],
                send_sem=send_sem.at[turn, 2 + side],
                recv_sem=recv_sem.at[turn, 2 + side],
                device_id=peers[2 + side],
                device_id_type=MESH,
            )
            copy.start()
            copies.append(copy)

        @pl.loop(0, tile_x)
        def _(row):
            x = row + PAD
            centre_weight = 1.0 - 4.0 * kappa[pl.ds(x, 1), :]
            for t in range(deep // SUB):
                at = pl.ds(pl.multiple_of(row * deep, SUB) + t * SUB, SUB)
                here = pl.ds(pl.multiple_of(x * deep, SUB) + t * SUB, SUB)
                e = [field[c, here, :] for c in range(4)]
                a, b, m, p = north_a[at, :], north_b[at, :], north_m[at, :], north_p[at, :]
                push = x_push(x, t)
                for c in range(4):
                    flow_a, flow_b, flow_m, flow_p = a * e[c], b * e[c], m * e[c], p * e[c]
                    if c < 2:
                        flow_a = flow_a + (pressure[c] * third * mask_a) * e[3]
                        flow_b = flow_b - (pressure[c] * third * mask_b) * e[3]
                        flow_m = flow_m + (pressure[c] * twelfth * mask_m) * e[3]
                        flow_p = flow_p + (pressure[c] * twelfth * mask_p) * e[3]
                    down_y = pltpu.roll(flow_a - pltpu.roll(flow_m, tile_y - 1, 1), tile_y - 1, 1)
                    up_y = pltpu.roll(flow_b + pltpu.roll(flow_p, 1, 1), 1, 1)
                    total = centre_weight * e[c] + x_part(c, x, t, push if c < 2 else None) + down_y + up_y
                    if c == 2:
                        total = total - cor * e[3]
                    if c == 3:
                        total = total + cor * e[2]
                    result[c, at, :] = total

        for copy in copies:
            copy.wait()

        from_east = (me_x < span_x - 1).astype(F32)
        from_west = (me_x > 0).astype(F32)
        for side, factor in ((0, from_east), (1, from_west)):
            for place in range(2):
                row = (tile_x - 2 + place) if side == 0 else place
                for c in range(4):
                    at = slice(row * deep, (row + 1) * deep)
                    result[c, at, :] = result[c, at, :] + factor * x_recv[turn, side, place, c]

        from_north = (me_y < span_y - 1).astype(F32)
        from_south = (me_y > 0).astype(F32)

        @pl.loop(0, rows // LANES)
        def _(part):
            here = pl.ds(pl.multiple_of(part * LANES, LANES), LANES)
            place = lax.broadcasted_iota(jnp.int32, (SUB, LANES), 0)
            got_north = y_recv[turn, 0, :, here] * from_north
            got_south = y_recv[turn, 1, :, here] * from_south
            for c in range(4):
                low = jnp.where(
                    place == 0, got_south[2 * c : 2 * c + 1, :], jnp.where(place == 1, got_south[2 * c + 1 : 2 * c + 2, :], 0.0)
                )
                high = jnp.where(
                    place == SUB - 2, got_north[2 * c : 2 * c + 1, :],
                    jnp.where(place == SUB - 1, got_north[2 * c + 1 : 2 * c + 2, :], 0.0),
                )
                whole = jnp.concatenate([low, jnp.zeros((tile_y - 2 * SUB, LANES), F32), high], axis=0)
                result[c, here, :] = result[c, here, :] + whole.T

    @pl.loop(0, levels)
    def _(l):
        under = l < wet
        for c in range(4):
            out_ref[c, l] = jnp.where(under, result[c, pl.ds(l, tile_x, stride=deep), :], 0.0)


def steps(state, forcing, velocity, diffusion, mixing, wet, deep, span_x, span_y):
    levels, tile_x, tile_y = state.shape[1:]
    rows = tile_x * deep
    wide = (tile_x + 2 * PAD) * deep
    vmem = pl.BlockSpec(memory_space=pltpu.VMEM)
    return pl.pallas_call(
        functools.partial(
            steps_kernel, levels=levels, deep=deep, span_x=span_x, span_y=span_y, total_rows=tile_y * span_y
        ),
        in_specs=[vmem] * 6,
        out_specs=vmem,
        out_shape=jax.ShapeDtypeStruct(state.shape, F32),
        scratch_shapes=[
            pltpu.VMEM((4, wide, tile_y), F32),
            pltpu.VMEM((wide, tile_y), F32),
            pltpu.VMEM((rows, tile_y), F32),
            pltpu.VMEM((rows, tile_y), F32),
            pltpu.VMEM((rows, tile_y), F32),
            pltpu.VMEM((rows, tile_y), F32),
            pltpu.VMEM((tile_x + 2 * PAD, tile_y), F32),
            pltpu.VMEM((4, rows, tile_y), F32),
            pltpu.VMEM((levels, tile_x, tile_y), F32),
            pltpu.VMEM((levels, tile_x, tile_y), F32),
            pltpu.VMEM((4, levels, tile_x, tile_y), F32),
            pltpu.VMEM((2, SUB, rows), F32),
            pltpu.VMEM((2, SUB, rows), F32),
            pltpu.VMEM((2, 2, 2, 4, deep, tile_y), F32),
            pltpu.VMEM((2, 2, 2, 4, deep, tile_y), F32),
            pltpu.VMEM((2, 2, SUB, rows), F32),
            pltpu.VMEM((2, 2, SUB, rows), F32),
            pltpu.SemaphoreType.DMA((2, 4)),
            pltpu.SemaphoreType.DMA((2, 4)),
        ],
        compiler_params=pltpu.CompilerParams(
            collective_id=0, has_side_effects=True, vmem_limit_bytes=56 << 20
        ),
        name="two_steps",
    )(state, forcing.reshape(-1, tile_y), velocity, diffusion, mixing, wet)


def on_device(
    adjoint_state, velocity, diffusivity, mixing, wet_levels, innovations, owner_tile, cell_index, offsets,
    live_counts, depth_weights,
):
    levels, tile_x, tile_y = adjoint_state.shape[1:]
    deep = -(-levels // SUB) * SUB
    span_x, span_y = lax.axis_size("gx"), lax.axis_size("gy")
    tiles = span_x * span_y
    sent = pack(
        innovations, owner_tile.reshape(1, -1), cell_index.reshape(1, -1), offsets, live_counts, depth_weights,
        tiles, levels, deep,
    )
    got = lax.all_to_all(sent.reshape(tiles, CAP, LANES), ("gx", "gy"), split_axis=0, concat_axis=0, tiled=True)
    forcing = scatter(got.reshape(tiles * CAP, LANES), tile_x, deep)
    return steps(adjoint_state, forcing, velocity, diffusivity, mixing, wet_levels, deep, span_x, span_y)


def solution(mesh):
    placed = (
        P(None, None, "gx", "gy"),
        P(None, None, "gx", "gy"),
        P("gx", "gy"),
        P("gx", "gy"),
        P("gx", "gy"),
        P(("gx", "gy"), None),
        P(("gx", "gy"), None),
        P(("gx", "gy")),
        P(None, ("gx", "gy")),
        P(("gx", "gy")),
        P(),
    )
    return jax.shard_map(
        on_device, mesh=mesh, in_specs=placed, out_specs=P(None, None, "gx", "gy"), check_vma=False
    )
```

```python
import functools

import jax
import jax.numpy as jnp
from jax import lax
from jax.experimental import pallas as pl
from jax.experimental.pallas import tpu as pltpu
from jax.sharding import PartitionSpec as P

F32 = jnp.float32
BF16 = jnp.bfloat16
MESH = pl.DeviceIdType.MESH

PRESSURE_HEAT = 0.2
PRESSURE_SALT = 0.15
CORIOLIS_PEAK = 0.2

CAP = 24
LANES = 128
SUB = 8
PAD = 4


def split(value):
    high = value.astype(BF16)
    return high, (value - high.astype(F32)).astype(BF16)


GROUP = 32
BURST = 8


def whole_kernel(
    live_ref, target_hbm, cell_hbm, offset_hbm, rows_hbm, weights_hbm, state_hbm, velocity_hbm, diffusion_hbm,
    mixing_hbm, wet_hbm, out_ref,
    target_ref, cell_ref, offset_ref, rows_ref, weights_ref, state_ref, velocity_ref, diffusion_ref, mixing_ref,
    wet_ref, packed, slots, send, recv, values, sides, columns, forcing_ref,
    field, east, north_a, north_b, north_m, north_p, kappa, result, inverse, gain, going,
    edge_lo, edge_hi, x_send, x_recv, y_send, y_recv,
    local_sem, row_send_sem, row_recv_sem, send_sem, recv_sem, ready_sem,
    *, levels, deep, span_x, span_y, total_rows,
):
    tile_x, tile_y = mixing_ref.shape
    rows = tile_x * deep
    tiles = span_x * span_y
    obs = rows_ref.shape[0]
    prof = weights_ref.shape[1]
    me_x, me_y = lax.axis_index("gx"), lax.axis_index("gy")
    west, right = lax.rem(me_x + span_x - 1, span_x), lax.rem(me_x + 1, span_x)
    south, up = lax.rem(me_y + span_y - 1, span_y), lax.rem(me_y + 1, span_y)
    peers = ((west, me_y), (right, me_y), (me_x, south), (me_x, up))

    moves = [
        pltpu.make_async_copy(source, target, local_sem.at[place])
        for place, (source, target) in enumerate(
            (
                (target_hbm, target_ref), (cell_hbm, cell_ref), (offset_hbm, offset_ref), (weights_hbm, weights_ref),
                (rows_hbm, rows_ref), (mixing_hbm, mixing_ref), (diffusion_hbm, diffusion_ref), (wet_hbm, wet_ref),
                (velocity_hbm, velocity_ref), (state_hbm, state_ref),
            )
        )
    ]
    for move in moves:
        move.start()

    barrier = pltpu.get_barrier_semaphore()
    row_peers = [(lax.rem(me_x + t, span_x), me_y) for t in range(1, span_x)]
    column_peers = [(me_x, lax.rem(me_y + t, span_y)) for t in range(1, span_y)]
    for peer in row_peers + column_peers:
        pl.semaphore_signal(barrier, inc=1, device_id=peer, device_id_type=MESH)

    for move in moves[:5]:
        move.wait()

    wide = jnp.concatenate([weights_ref[...], jnp.zeros((levels, LANES - prof), F32)], axis=1)
    gap = jnp.zeros((deep - levels, LANES), F32)
    both = jnp.concatenate(
        [wide, gap, pltpu.roll(wide, prof, 1), gap, jnp.zeros((LANES - 2 * deep, LANES), F32)], axis=0
    ).T
    tri = (
        lax.broadcasted_iota(jnp.int32, (256, 256), 0) < lax.broadcasted_iota(jnp.int32, (256, 256), 1)
    ).astype(BF16)
    tile_place = lax.broadcasted_iota(jnp.int32, (tiles, 256), 0)
    carry = jnp.zeros((tiles, 1), F32)
    for part in range(obs // 256):
        span = slice(part * 256, (part + 1) * 256)
        place = lax.broadcasted_iota(jnp.int32, (1, 256), 1) + part * 256
        live = place < live_ref[0]
        target = target_ref[:, span]
        named = ((tile_place == target) & live).astype(F32)
        before = jnp.dot(named.astype(BF16), tri, preferred_element_type=F32) + carry
        rank = jnp.sum(named * before, axis=0, keepdims=True)
        carry = carry + jnp.sum(named, axis=1, keepdims=True)
        slots[:, span] = jnp.where(live, target * CAP + rank.astype(jnp.int32), -1)
        cell = cell_ref[:, span].astype(F32)
        cell_row = jnp.floor((cell + 0.5) * (1.0 / (tile_y - 1)))
        cell_col = cell - (tile_y - 1.0) * cell_row
        for half in range(2):
            cut = slice(half * LANES, (half + 1) * LANES)
            here = slice(part * 256 + half * LANES, part * 256 + (half + 1) * LANES)
            side = jnp.concatenate(
                [
                    jnp.zeros((2 * deep, LANES), F32), cell_row[:, cut], cell_col[:, cut], offset_ref[:, here],
                    jnp.zeros((LANES - 2 * deep - 4, LANES), F32),
                ],
                axis=0,
            )
            profile = jnp.dot(rows_ref[here, :], both, precision=lax.Precision.HIGHEST, preferred_element_type=F32)
            high, low = split(profile + side.T)
            packed[here, :LANES] = high
            packed[here, LANES:] = low

    pl.semaphore_wait(barrier, len(row_peers) + len(column_peers))
    for peer in column_peers:
        pl.semaphore_signal(ready_sem, inc=1, device_id=peer, device_id_type=MESH)
    pl.semaphore_wait(ready_sem, len(column_peers))

    def peer_of(t):
        dx = lax.rem(t, span_x)
        return lax.rem(me_x + dx, span_x), lax.rem(me_y + t // span_x + 2 * dx, span_y)

    def row_copy(t):
        return pltpu.make_async_remote_copy(
            src_ref=send.at[t], dst_ref=recv.at[t], send_sem=row_send_sem, recv_sem=row_recv_sem.at[t // GROUP],
            device_id=peer_of(t), device_id_type=MESH,
        )

    @pl.loop(0, tiles // BURST)
    def _(burst):
        places = []
        for r in range(BURST):
            peer_x, peer_y = peer_of(burst * BURST + r)
            base = (peer_x * span_y + peer_y) * CAP
            places.append(lax.broadcasted_iota(jnp.int32, (CAP, 1), 0) + base)
        pick = (jnp.concatenate(places, axis=0) == slots[...]).astype(F32).astype(BF16)
        got = jnp.dot(pick, packed[...], preferred_element_type=F32)
        got = got[:, :LANES] + got[:, LANES:]
        for r in range(BURST):
            send[burst * BURST + r] = got[r * CAP : (r + 1) * CAP]
        for r in range(BURST):
            if r == 0:

                @pl.when(burst > 0)
                def _():
                    row_copy(burst * BURST).start()

                @pl.when(burst == 0)
                def _():
                    recv[0] = got[:CAP]
            else:
                row_copy(burst * BURST + r).start()

    for move in moves[5:9]:
        move.wait()
    mixing = mixing_ref[...]
    lane = lax.broadcasted_iota(jnp.int32, (1, tile_y), 1)
    third, twelfth = 8.0 / 12.0, 1.0 / 12.0

    def coefficient(l, q_before):
        diag = 1.0 + mixing * jnp.where((l == 0) | (l == levels - 1), 1.0, 2.0)
        q = 1.0 / (diag - mixing * mixing * q_before)
        inverse[l] = q
        gain[l] = mixing * q
        return q

    lax.fori_loop(0, levels, coefficient, jnp.zeros_like(mixing))

    zero_rows = jnp.zeros((PAD * deep, tile_y), F32)
    for c in range(4):
        field[c, : PAD * deep, :] = zero_rows
        field[c, (PAD + tile_x) * deep :, :] = zero_rows
    east[: PAD * deep, :] = zero_rows
    east[(PAD + tile_x) * deep :, :] = zero_rows
    kappa[...] = jnp.zeros_like(kappa)
    kappa[PAD : PAD + tile_x, :] = diffusion_ref[...]

    @pl.loop(0, deep - levels)
    def _(extra):
        blank = jnp.zeros((tile_x, tile_y), F32)
        for c in range(4):
            field[c, pl.ds(PAD * deep + levels + extra, tile_x, stride=deep), :] = blank
            result[c, pl.ds(levels + extra, tile_x, stride=deep), :] = blank
        east[pl.ds(PAD * deep + levels + extra, tile_x, stride=deep), :] = blank
        for table in (north_a, north_b, north_m, north_p):
            table[pl.ds(levels + extra, tile_x, stride=deep), :] = blank

    diffusion = diffusion_ref[...]
    mask_a = (lane >= 1).astype(F32)
    mask_b = (lane < tile_y - 1).astype(F32)
    mask_m = (lane >= 2).astype(F32)
    mask_p = (lane < tile_y - 2).astype(F32)

    @pl.loop(0, levels)
    def _(l):
        u, v = velocity_ref[0, l], velocity_ref[1, l]
        east[pl.ds(PAD * deep + l, tile_x, stride=deep), :] = u
        here = pl.ds(l, tile_x, stride=deep)
        north_a[here, :] = (third * v + diffusion) * mask_a
        north_b[here, :] = (diffusion - third * v) * mask_b
        north_m[here, :] = (twelfth * v) * mask_m
        north_p[here, :] = (twelfth * v) * mask_p

    @pl.loop(0, rows // LANES)
    def _(part):
        here = pl.ds(pl.multiple_of(part * LANES, LANES), LANES)
        edge_lo[0, :, here] = north_b[here, :].T[:SUB, :]
        edge_lo[1, :, here] = north_p[here, :].T[:SUB, :]
        edge_hi[0, :, here] = north_a[here, :].T[tile_y - SUB :, :]
        edge_hi[1, :, here] = north_m[here, :].T[tile_y - SUB :, :]

    cor = CORIOLIS_PEAK * (2.0 * ((lane + me_y * tile_y).astype(F32) + 0.5) / total_rows - 1.0)
    wet = wet_ref[...]
    pressure = (PRESSURE_HEAT, -PRESSURE_SALT)

    def x_part(c, x, t, push):
        def at(shift):
            return pl.ds(pl.multiple_of((x + shift) * deep, SUB) + t * SUB, SUB)

        def coef(shift):
            return third * east[at(shift), :], kappa[pl.ds(x + shift, 1), :]

        (flow_up, kap_up), (flow_down, kap_down) = coef(1), coef(-1)
        total = (
            (flow_up + kap_up) * field[c, at(1), :]
            + (kap_down - flow_down) * field[c, at(-1), :]
            - twelfth * (east[at(2), :] * field[c, at(2), :] - east[at(-2), :] * field[c, at(-2), :])
        )
        return total if push is None else total + pressure[c] * push

    def x_push(x, t):
        def at(shift):
            return pl.ds(pl.multiple_of((x + shift) * deep, SUB) + t * SUB, SUB)

        return third * (field[2, at(1), :] - field[2, at(-1), :]) - twelfth * (field[2, at(2), :] - field[2, at(-2), :])


    forcing_ref[...] = jnp.zeros_like(forcing_ref)
    count = GROUP * CAP
    y_place = lax.broadcasted_iota(jnp.int32, (tile_y, LANES), 0).astype(F32)
    for group in range(tiles // GROUP):
        first = 1 if group == 0 else 0
        came = pl.ds(group * GROUP + first, GROUP - first)
        pltpu.make_async_remote_copy(
            src_ref=send.at[came], dst_ref=recv.at[came], send_sem=row_send_sem, recv_sem=row_recv_sem.at[group],
            device_id=peers[0], device_id_type=MESH,
        ).wait_recv()
        table = recv[group * GROUP : (group + 1) * GROUP].reshape(count, LANES)
        for part in range(count // LANES):
            here = slice(part * LANES, (part + 1) * LANES)
            turned = table[here].T
            high, low = split(turned[: 2 * deep])
            values[: 2 * deep, here] = high
            values[2 * deep :, here] = low
            side = turned[2 * deep : 2 * deep + SUB]
            sides[:, here] = side
            col, north = side[1:2, :], side[3:4, :]
            columns[:, here] = jnp.where(y_place == col, 1.0 - north, 0.0) + jnp.where(y_place == col + 1.0, north, 0.0)

        @pl.loop(0, tile_x // 2)
        def _(pair):
            cell_row, aside = sides[0:1, :], sides[2:3, :]
            high, low = [], []
            for half in range(2):
                x_now = (2 * pair + half).astype(F32)
                share = jnp.where(cell_row == x_now, 1.0 - aside, 0.0) + jnp.where(cell_row + 1.0 == x_now, aside, 0.0)
                one, two = split(columns[...] * share)
                high.append(one)
                low.append(two)
            across = (((1,), (1,)), ((), ()))
            got = lax.dot_general(values[...], jnp.concatenate(high, axis=0), across, preferred_element_type=F32)
            rest = lax.dot_general(
                values[: 2 * deep], jnp.concatenate(low, axis=0), across, preferred_element_type=F32
            )
            total = got[: 2 * deep] + got[2 * deep :] + rest
            for half in range(2):
                at = pl.ds(pl.multiple_of((2 * pair + half) * (2 * deep), SUB), 2 * deep)
                forcing_ref[at, :] = forcing_ref[at, :] + total[:, half * tile_y : (half + 1) * tile_y]

    sent = pl.ds(1, tiles - 1)
    pltpu.make_async_remote_copy(
        src_ref=send.at[sent], dst_ref=recv.at[sent], send_sem=row_send_sem, recv_sem=row_recv_sem.at[0],
        device_id=peers[0], device_id_type=MESH,
    ).wait_send()
    moves[9].wait()

    for turn in range(2):
        def down(l, before):
            now = []
            q, p = inverse[l], gain[l]
            under = l < wet
            for c in range(4):
                if turn == 0:
                    value = state_ref[c, l]
                    if c < 2:
                        value = value + forcing_ref[pl.ds(c * deep + l, tile_x, stride=2 * deep), :]
                else:
                    value = result[c, pl.ds(l, tile_x, stride=deep), :]
                value = jnp.where(under, value, 0.0) * q + p * before[c]
                going[c, l] = value
                now.append(value)
            return tuple(now)

        lax.fori_loop(0, levels, down, (jnp.zeros((tile_x, tile_y), F32),) * 4)

        def rise(k, below):
            l = levels - 1 - k
            p = jnp.where(k == 0, 0.0, 1.0) * gain[l]
            now = []
            for c in range(4):
                value = going[c, l] + p * below[c]
                field[c, pl.ds(PAD * deep + l, tile_x, stride=deep), :] = value
                now.append(value)
            return tuple(now)

        lax.fori_loop(0, levels, rise, (jnp.zeros((tile_x, tile_y), F32),) * 4)

        copies = []
        for side in range(2):
            for place in range(2):
                x = (PAD - 2 + place) if side == 0 else (PAD + tile_x + place)
                for t in range(deep // SUB):
                    push = x_push(x, t)
                    for c in range(4):
                        x_send[turn, side, place, c, t * SUB : (t + 1) * SUB, :] = x_part(c, x, t, push if c < 2 else None)
            copy = pltpu.make_async_remote_copy(
                src_ref=x_send.at[turn, side],
                dst_ref=x_recv.at[turn, side],
                send_sem=send_sem.at[turn, side],
                recv_sem=recv_sem.at[turn, side],
                device_id=peers[side],
                device_id_type=MESH,
            )
            copy.start()
            copies.append(copy)

        @pl.loop(0, rows // LANES)
        def _(part):
            here = pl.ds(pl.multiple_of(part * LANES, LANES), LANES)
            there = pl.ds(pl.multiple_of(part * LANES + PAD * deep, SUB), LANES)
            turned = [field[c, there, :].T for c in range(4)]
            b_lo, c_lo = edge_lo[0, :, here], edge_lo[1, :, here]
            a_hi, c_hi = edge_hi[0, :, here], edge_hi[1, :, here]
            a_lo, b_hi = b_lo + 16.0 * c_lo, a_hi - 16.0 * c_hi
            e_lo = [value[:SUB, :] for value in turned]
            e_hi = [value[tile_y - SUB :, :] for value in turned]
            for c in range(4):
                flow_a, flow_c = a_lo * e_lo[c], c_lo * e_lo[c]
                flow_b, flow_d = b_hi * e_hi[c], c_hi * e_hi[c]
                if c < 2:
                    flow_a = flow_a + pressure[c] * third * e_lo[3]
                    flow_c = flow_c + pressure[c] * twelfth * e_lo[3]
                    flow_b = flow_b - pressure[c] * third * e_hi[3]
                    flow_d = flow_d + pressure[c] * twelfth * e_hi[3]
                y_send[turn, 0, 2 * c : 2 * c + 1, here] = -flow_c[0:1, :]
                y_send[turn, 0, 2 * c + 1 : 2 * c + 2, here] = flow_a[0:1, :] - flow_c[1:2, :]
                y_send[turn, 1, 2 * c : 2 * c + 1, here] = flow_b[7:8, :] + flow_d[6:7, :]
                y_send[turn, 1, 2 * c + 1 : 2 * c + 2, here] = flow_d[7:8, :]

        for side in range(2):
            copy = pltpu.make_async_remote_copy(
                src_ref=y_send.at[turn, side],
                dst_ref=y_recv.at[turn, side],
                send_sem=send_sem.at[turn, 2 + side],
                recv_sem=recv_sem.at[turn, 2 + side],
                device_id=peers[2 + side],
                device_id_type=MESH,
            )
            copy.start()
            copies.append(copy)

        @pl.loop(0, tile_x)
        def _(row):
            x = row + PAD
            centre_weight = 1.0 - 4.0 * kappa[pl.ds(x, 1), :]
            for t in range(deep // SUB):
                at = pl.ds(pl.multiple_of(row * deep, SUB) + t * SUB, SUB)
                here = pl.ds(pl.multiple_of(x * deep, SUB) + t * SUB, SUB)
                e = [field[c, here, :] for c in range(4)]
                a, b, m, p = north_a[at, :], north_b[at, :], north_m[at, :], north_p[at, :]
                push = x_push(x, t)
                for c in range(4):
                    flow_a, flow_b, flow_m, flow_p = a * e[c], b * e[c], m * e[c], p * e[c]
                    if c < 2:
                        flow_a = flow_a + (pressure[c] * third * mask_a) * e[3]
                        flow_b = flow_b - (pressure[c] * third * mask_b) * e[3]
                        flow_m = flow_m + (pressure[c] * twelfth * mask_m) * e[3]
                        flow_p = flow_p + (pressure[c] * twelfth * mask_p) * e[3]
                    down_y = pltpu.roll(flow_a - pltpu.roll(flow_m, tile_y - 1, 1), tile_y - 1, 1)
                    up_y = pltpu.roll(flow_b + pltpu.roll(flow_p, 1, 1), 1, 1)
                    total = centre_weight * e[c] + x_part(c, x, t, push if c < 2 else None) + down_y + up_y
                    if c == 2:
                        total = total - cor * e[3]
                    if c == 3:
                        total = total + cor * e[2]
                    result[c, at, :] = total

        for copy in copies:
            copy.wait()

        from_east = (me_x < span_x - 1).astype(F32)
        from_west = (me_x > 0).astype(F32)
        for side, factor in ((0, from_east), (1, from_west)):
            for place in range(2):
                row = (tile_x - 2 + place) if side == 0 else place
                for c in range(4):
                    at = slice(row * deep, (row + 1) * deep)
                    result[c, at, :] = result[c, at, :] + factor * x_recv[turn, side, place, c]

        from_north = (me_y < span_y - 1).astype(F32)
        from_south = (me_y > 0).astype(F32)

        @pl.loop(0, rows // LANES)
        def _(part):
            here = pl.ds(pl.multiple_of(part * LANES, LANES), LANES)
            place = lax.broadcasted_iota(jnp.int32, (SUB, LANES), 0)
            got_north = y_recv[turn, 0, :, here] * from_north
            got_south = y_recv[turn, 1, :, here] * from_south
            for c in range(4):
                low = jnp.where(
                    place == 0, got_south[2 * c : 2 * c + 1, :], jnp.where(place == 1, got_south[2 * c + 1 : 2 * c + 2, :], 0.0)
                )
                high = jnp.where(
                    place == SUB - 2, got_north[2 * c : 2 * c + 1, :],
                    jnp.where(place == SUB - 1, got_north[2 * c + 1 : 2 * c + 2, :], 0.0),
                )
                whole = jnp.concatenate([low, jnp.zeros((tile_y - 2 * SUB, LANES), F32), high], axis=0)
                result[c, here, :] = result[c, here, :] + whole.T

    @pl.loop(0, levels)
    def _(l):
        under = l < wet
        for c in range(4):
            out_ref[c, l] = jnp.where(under, result[c, pl.ds(l, tile_x, stride=deep), :], 0.0)


def on_device(
    adjoint_state, velocity, diffusivity, mixing, wet_levels, innovations, owner_tile, cell_index, offsets,
    live_counts, depth_weights,
):
    levels, tile_x, tile_y = adjoint_state.shape[1:]
    deep = -(-levels // SUB) * SUB
    span_x, span_y = lax.axis_size("gx"), lax.axis_size("gy")
    tiles = span_x * span_y
    obs = innovations.shape[0]
    prof = depth_weights.shape[0]
    rows = tile_x * deep
    wide = (tile_x + 2 * PAD) * deep
    hbm = pl.BlockSpec(memory_space=pltpu.HBM)
    vmem = lambda *shape: pltpu.VMEM(shape, F32)
    return pl.pallas_call(
        functools.partial(
            whole_kernel, levels=levels, deep=deep, span_x=span_x, span_y=span_y, total_rows=tile_y * span_y
        ),
        in_specs=[pl.BlockSpec(memory_space=pltpu.SMEM)] + [hbm] * 10,
        out_specs=pl.BlockSpec(memory_space=pltpu.VMEM),
        out_shape=jax.ShapeDtypeStruct(adjoint_state.shape, F32),
        scratch_shapes=[
            pltpu.VMEM((1, obs), jnp.int32),
            pltpu.VMEM((1, obs), jnp.int32),
            vmem(2, obs),
            vmem(obs, LANES),
            vmem(levels, prof),
            vmem(4, levels, tile_x, tile_y),
            vmem(2, levels, tile_x, tile_y),
            vmem(tile_x, tile_y),
            vmem(tile_x, tile_y),
            pltpu.VMEM((tile_x, tile_y), jnp.int32),
            pltpu.VMEM((obs, 2 * LANES), BF16),
            pltpu.VMEM((1, obs), jnp.int32),
            vmem(tiles, CAP, LANES),
            vmem(tiles, CAP, LANES),
            pltpu.VMEM((4 * deep, GROUP * CAP), BF16),
            vmem(SUB, GROUP * CAP),
            vmem(tile_y, GROUP * CAP),
            vmem(tile_x * 2 * deep, tile_y),
            vmem(4, wide, tile_y),
            vmem(wide, tile_y),
            vmem(rows, tile_y),
            vmem(rows, tile_y),
            vmem(rows, tile_y),
            vmem(rows, tile_y),
            vmem(tile_x + 2 * PAD, tile_y),
            vmem(4, rows, tile_y),
            vmem(levels, tile_x, tile_y),
            vmem(levels, tile_x, tile_y),
            vmem(4, levels, tile_x, tile_y),
            vmem(2, SUB, rows),
            vmem(2, SUB, rows),
            vmem(2, 2, 2, 4, deep, tile_y),
            vmem(2, 2, 2, 4, deep, tile_y),
            vmem(2, 2, SUB, rows),
            vmem(2, 2, SUB, rows),
            pltpu.SemaphoreType.DMA((10,)),
            pltpu.SemaphoreType.DMA,
            pltpu.SemaphoreType.DMA((tiles // GROUP,)),
            pltpu.SemaphoreType.DMA((2, 4)),
            pltpu.SemaphoreType.DMA((2, 4)),
            pltpu.SemaphoreType.REGULAR,
        ],
        compiler_params=pltpu.CompilerParams(collective_id=0, has_side_effects=True, vmem_limit_bytes=60 << 20),
        name="whole",
    )(
        live_counts, owner_tile.reshape(1, obs), cell_index.reshape(1, obs), offsets, innovations, depth_weights.T,
        adjoint_state, velocity, diffusivity, mixing, wet_levels,
    )


def solution(mesh):
    placed = (
        P(None, None, "gx", "gy"),
        P(None, None, "gx", "gy"),
        P("gx", "gy"),
        P("gx", "gy"),
        P("gx", "gy"),
        P(("gx", "gy"), None),
        P(("gx", "gy"), None),
        P(("gx", "gy")),
        P(None, ("gx", "gy")),
        P(("gx", "gy")),
        P(),
    )
    return jax.shard_map(
        on_device, mesh=mesh, in_specs=placed, out_specs=P(None, None, "gx", "gy"), check_vma=False
    )
```

```python
import functools

import jax
import jax.numpy as jnp
from jax import lax
from jax.experimental import pallas as pl
from jax.experimental.pallas import tpu as pltpu
from jax.sharding import PartitionSpec as P

F32 = jnp.float32
BF16 = jnp.bfloat16
MESH = pl.DeviceIdType.MESH

PRESSURE_HEAT = 0.2
PRESSURE_SALT = 0.15
CORIOLIS_PEAK = 0.2

CAP = 24
LANES = 128
SUB = 8
PAD = 4


def split(value):
    high = value.astype(BF16)
    return high, (value - high.astype(F32)).astype(BF16)


GROUP = 32
BURST = 8
AHEAD = 3


def whole_kernel(
    live_ref, target_hbm, cell_hbm, offset_hbm, rows_hbm, weights_hbm, state_hbm, velocity_hbm, diffusion_hbm,
    mixing_hbm, wet_hbm, out_ref,
    target_ref, cell_ref, offset_ref, rows_ref, weights_ref, state_ref, velocity_ref, diffusion_ref, mixing_ref,
    wet_ref, packed, slots, send, recv, values, sides, columns, forcing_ref,
    field, east_a, east_b, east_c, north_a, north_b, north_m, north_p, kappa, result, inverse, gain, going,
    edge_lo, edge_hi, x_send, x_recv, y_send, y_recv,
    local_sem, row_send_sem, row_recv_sem, send_sem, recv_sem,
    *, levels, deep, span_x, span_y, total_rows,
):
    tile_x, tile_y = mixing_ref.shape
    rows = tile_x * deep
    tiles = span_x * span_y
    obs = rows_ref.shape[0]
    prof = weights_ref.shape[1]
    me_x, me_y = lax.axis_index("gx"), lax.axis_index("gy")
    west, right = lax.rem(me_x + span_x - 1, span_x), lax.rem(me_x + 1, span_x)
    south, up = lax.rem(me_y + span_y - 1, span_y), lax.rem(me_y + 1, span_y)
    peers = ((west, me_y), (right, me_y), (me_x, south), (me_x, up))

    moves = [
        pltpu.make_async_copy(source, target, local_sem.at[place])
        for place, (source, target) in enumerate(
            (
                (target_hbm, target_ref), (cell_hbm, cell_ref), (offset_hbm, offset_ref), (weights_hbm, weights_ref),
                (rows_hbm, rows_ref), (mixing_hbm, mixing_ref), (diffusion_hbm, diffusion_ref), (wet_hbm, wet_ref),
                (velocity_hbm, velocity_ref), (state_hbm, state_ref),
            )
        )
    ]
    for move in moves:
        move.start()

    others = [
        (lax.rem(me_x + t % span_x, span_x), lax.rem(me_y + t // span_x + 2 * (t % span_x), span_y))
        for t in range(1, tiles)
    ]
    barrier = pltpu.get_barrier_semaphore()
    for other in others:
        pl.semaphore_signal(barrier, inc=1, device_id=other, device_id_type=MESH)

    for move in moves[:5]:
        move.wait()

    wide = jnp.concatenate([weights_ref[...], jnp.zeros((levels, LANES - prof), F32)], axis=1)
    gap = jnp.zeros((deep - levels, LANES), F32)
    both = jnp.concatenate(
        [wide, gap, pltpu.roll(wide, prof, 1), gap, jnp.zeros((LANES - 2 * deep, LANES), F32)], axis=0
    ).T
    tri = (
        lax.broadcasted_iota(jnp.int32, (256, 256), 0) < lax.broadcasted_iota(jnp.int32, (256, 256), 1)
    ).astype(BF16)
    tile_place = lax.broadcasted_iota(jnp.int32, (tiles, 256), 0)
    carry = jnp.zeros((tiles, 1), F32)
    for part in range(obs // 256):
        span = slice(part * 256, (part + 1) * 256)
        place = lax.broadcasted_iota(jnp.int32, (1, 256), 1) + part * 256
        live = place < live_ref[0]
        target = target_ref[:, span]
        named = ((tile_place == target) & live).astype(F32)
        before = jnp.dot(named.astype(BF16), tri, preferred_element_type=F32) + carry
        rank = jnp.sum(named * before, axis=0, keepdims=True)
        carry = carry + jnp.sum(named, axis=1, keepdims=True)
        slots[:, span] = jnp.where(live, target * CAP + rank.astype(jnp.int32), -1)
        cell = cell_ref[:, span].astype(F32)
        cell_row = jnp.floor((cell + 0.5) * (1.0 / (tile_y - 1)))
        cell_col = cell - (tile_y - 1.0) * cell_row
        for half in range(2):
            cut = slice(half * LANES, (half + 1) * LANES)
            here = slice(part * 256 + half * LANES, part * 256 + (half + 1) * LANES)
            side = jnp.concatenate(
                [
                    jnp.zeros((2 * deep, LANES), F32), cell_row[:, cut], cell_col[:, cut], offset_ref[:, here],
                    jnp.zeros((LANES - 2 * deep - 4, LANES), F32),
                ],
                axis=0,
            )
            profile = jnp.dot(rows_ref[here, :], both, precision=lax.Precision.HIGHEST, preferred_element_type=F32)
            high, low = split(profile + side.T)
            packed[here, :LANES] = high
            packed[here, LANES:] = low

    def send_burst(burst):
        for t in range(burst * BURST, min((burst + 1) * BURST, len(others))):
            pltpu.make_async_remote_copy(
                src_ref=send.at[t], dst_ref=recv.at[t], send_sem=row_send_sem, recv_sem=row_recv_sem.at[t // GROUP],
                device_id=others[t], device_id_type=MESH,
            ).start()

    named_tiles = others + [(me_x, me_y)]
    for burst in range(tiles // BURST):
        cut = slice(burst * BURST, (burst + 1) * BURST)
        slot = lax.broadcasted_iota(jnp.int32, (CAP, 1), 0)
        place = jnp.concatenate([slot + (x * span_y + y) * CAP for x, y in named_tiles[cut]], axis=0)
        pick = (place == slots[...]).astype(F32).astype(BF16)
        got = jnp.dot(pick, packed[...], preferred_element_type=F32)
        got = got[:, :LANES] + got[:, LANES:]
        send[cut] = got.reshape(BURST, CAP, LANES)
        if burst == AHEAD - 1:
            pl.semaphore_wait(barrier, len(others))
            for early in range(AHEAD):
                send_burst(early)
        if burst >= AHEAD:
            send_burst(burst)
    recv[tiles - 1] = send[tiles - 1]

    for move in moves[5:9]:
        move.wait()
    mixing = mixing_ref[...]
    lane = lax.broadcasted_iota(jnp.int32, (1, tile_y), 1)
    third, twelfth = 8.0 / 12.0, 1.0 / 12.0

    def coefficient(l, q_before):
        diag = 1.0 + mixing * jnp.where((l == 0) | (l == levels - 1), 1.0, 2.0)
        q = 1.0 / (diag - mixing * mixing * q_before)
        inverse[l] = q
        gain[l] = mixing * q
        return q

    lax.fori_loop(0, levels, coefficient, jnp.zeros_like(mixing))

    zero_rows = jnp.zeros((PAD * deep, tile_y), F32)
    for c in range(4):
        field[c, : PAD * deep, :] = zero_rows
        field[c, (PAD + tile_x) * deep :, :] = zero_rows
    for table in (east_a, east_b, east_c):
        table[: PAD * deep, :] = zero_rows
        table[(PAD + tile_x) * deep :, :] = zero_rows
    kappa[...] = jnp.zeros_like(kappa)
    kappa[PAD : PAD + tile_x, :] = diffusion_ref[...]

    @pl.loop(0, deep - levels)
    def _(extra):
        blank = jnp.zeros((tile_x, tile_y), F32)
        for c in range(4):
            field[c, pl.ds(PAD * deep + levels + extra, tile_x, stride=deep), :] = blank
            result[c, pl.ds(levels + extra, tile_x, stride=deep), :] = blank
        for table in (east_a, east_b, east_c):
            table[pl.ds(PAD * deep + levels + extra, tile_x, stride=deep), :] = blank
        for table in (north_a, north_b, north_m, north_p):
            table[pl.ds(levels + extra, tile_x, stride=deep), :] = blank

    diffusion = diffusion_ref[...]
    mask_a = (lane >= 1).astype(F32)
    mask_b = (lane < tile_y - 1).astype(F32)
    mask_m = (lane >= 2).astype(F32)
    mask_p = (lane < tile_y - 2).astype(F32)

    @pl.loop(0, levels)
    def _(l):
        u, v = velocity_ref[0, l], velocity_ref[1, l]
        there = pl.ds(PAD * deep + l, tile_x, stride=deep)
        east_a[there, :] = third * u + diffusion
        east_b[there, :] = diffusion - third * u
        east_c[there, :] = twelfth * u
        here = pl.ds(l, tile_x, stride=deep)
        north_a[here, :] = (third * v + diffusion) * mask_a
        north_b[here, :] = (diffusion - third * v) * mask_b
        north_m[here, :] = (twelfth * v) * mask_m
        north_p[here, :] = (twelfth * v) * mask_p

    @pl.loop(0, rows // LANES)
    def _(part):
        here = pl.ds(pl.multiple_of(part * LANES, LANES), LANES)
        edge_lo[0, :, here] = north_b[here, :].T[:SUB, :]
        edge_lo[1, :, here] = north_p[here, :].T[:SUB, :]
        edge_hi[0, :, here] = north_a[here, :].T[tile_y - SUB :, :]
        edge_hi[1, :, here] = north_m[here, :].T[tile_y - SUB :, :]

    cor = CORIOLIS_PEAK * (2.0 * ((lane + me_y * tile_y).astype(F32) + 0.5) / total_rows - 1.0)
    full = (SUB, tile_y)
    cor = jnp.broadcast_to(cor, full)
    wide_a, wide_b = jnp.broadcast_to(third * mask_a, full), jnp.broadcast_to(third * mask_b, full)
    wide_m, wide_p = jnp.broadcast_to(twelfth * mask_m, full), jnp.broadcast_to(twelfth * mask_p, full)
    wet = wet_ref[...]
    pressure = (PRESSURE_HEAT, -PRESSURE_SALT)

    def x_parts(x, t):
        def at(shift):
            return pl.ds(pl.multiple_of((x + shift) * deep, SUB) + t * SUB, SUB)

        up_1, down_1, up_2, down_2 = at(1), at(-1), at(2), at(-2)
        a, b, c_up, c_down = east_a[up_1, :], east_b[down_1, :], east_c[up_2, :], east_c[down_2, :]
        totals = []
        for c in range(4):
            e_up, e_down, e_up_2, e_down_2 = (field[c, place, :] for place in (up_1, down_1, up_2, down_2))
            totals.append((a * e_up + b * e_down) + (c_down * e_down_2 - c_up * e_up_2))
            if c == 2:
                push = third * (e_up - e_down) - twelfth * (e_up_2 - e_down_2)
        return [totals[0] + pressure[0] * push, totals[1] + pressure[1] * push, totals[2], totals[3]]

    forcing_ref[...] = jnp.zeros_like(forcing_ref)
    count = GROUP * CAP
    y_place = lax.broadcasted_iota(jnp.int32, (tile_y, LANES), 0).astype(F32)
    for group in range(tiles // GROUP):
        came = pl.ds(group * GROUP, min(GROUP, len(others) - group * GROUP))
        pltpu.make_async_remote_copy(
            src_ref=send.at[came], dst_ref=recv.at[came], send_sem=row_send_sem, recv_sem=row_recv_sem.at[group],
            device_id=peers[0], device_id_type=MESH,
        ).wait_recv()
        table = recv[group * GROUP : (group + 1) * GROUP].reshape(count, LANES)
        for part in range(count // LANES):
            here = slice(part * LANES, (part + 1) * LANES)
            turned = table[here].T
            high, low = split(turned[: 2 * deep])
            values[: 2 * deep, here] = high
            values[2 * deep :, here] = low
            side = turned[2 * deep : 2 * deep + SUB]
            sides[:, here] = side
            col, north = side[1:2, :], side[3:4, :]
            columns[:, here] = jnp.where(y_place == col, 1.0 - north, 0.0) + jnp.where(y_place == col + 1.0, north, 0.0)

        @pl.loop(0, tile_x // 2)
        def _(pair):
            cell_row, aside = sides[0:1, :], sides[2:3, :]
            high, low = [], []
            for half in range(2):
                x_now = (2 * pair + half).astype(F32)
                share = jnp.where(cell_row == x_now, 1.0 - aside, 0.0) + jnp.where(cell_row + 1.0 == x_now, aside, 0.0)
                one, two = split(columns[...] * share)
                high.append(one)
                low.append(two)
            across = (((1,), (1,)), ((), ()))
            got = lax.dot_general(values[...], jnp.concatenate(high, axis=0), across, preferred_element_type=F32)
            rest = lax.dot_general(
                values[: 2 * deep], jnp.concatenate(low, axis=0), across, preferred_element_type=F32
            )
            total = got[: 2 * deep] + got[2 * deep :] + rest
            for half in range(2):
                at = pl.ds(pl.multiple_of((2 * pair + half) * (2 * deep), SUB), 2 * deep)
                forcing_ref[at, :] = forcing_ref[at, :] + total[:, half * tile_y : (half + 1) * tile_y]

    sent = pl.ds(0, len(others))
    pltpu.make_async_remote_copy(
        src_ref=send.at[sent], dst_ref=recv.at[sent], send_sem=row_send_sem, recv_sem=row_recv_sem.at[0],
        device_id=peers[0], device_id_type=MESH,
    ).wait_send()
    moves[9].wait()

    def fives(body):
        def run(k, carry):
            for one in range(5):
                carry = body(5 * k + one, carry)
            return carry

        return run

    for turn in range(2):
        def down(l, before):
            now = []
            q, p = inverse[l], gain[l]
            under = l < wet
            for c in range(4):
                if turn == 0:
                    value = state_ref[c, l]
                    if c < 2:
                        value = value + forcing_ref[pl.ds(c * deep + l, tile_x, stride=2 * deep), :]
                else:
                    value = result[c, pl.ds(l, tile_x, stride=deep), :]
                value = jnp.where(under, value, 0.0) * q + p * before[c]
                going[c, l] = value
                now.append(value)
            return tuple(now)

        lax.fori_loop(0, levels // 5, fives(down), (jnp.zeros((tile_x, tile_y), F32),) * 4)

        def rise(k, below):
            l = levels - 1 - k
            p = jnp.where(k == 0, 0.0, 1.0) * gain[l]
            now = []
            for c in range(4):
                value = going[c, l] + p * below[c]
                field[c, pl.ds(PAD * deep + l, tile_x, stride=deep), :] = value
                now.append(value)
            return tuple(now)

        lax.fori_loop(0, levels // 5, fives(rise), (jnp.zeros((tile_x, tile_y), F32),) * 4)

        copies = []
        for side in range(2):
            for place in range(2):
                x = (PAD - 2 + place) if side == 0 else (PAD + tile_x + place)
                for t in range(deep // SUB):
                    for c, part in enumerate(x_parts(x, t)):
                        x_send[turn, side, place, c, t * SUB : (t + 1) * SUB, :] = part
            copy = pltpu.make_async_remote_copy(
                src_ref=x_send.at[turn, side],
                dst_ref=x_recv.at[turn, side],
                send_sem=send_sem.at[turn, side],
                recv_sem=recv_sem.at[turn, side],
                device_id=peers[side],
                device_id_type=MESH,
            )
            copy.start()
            copies.append(copy)

        @pl.loop(0, rows // LANES)
        def _(part):
            here = pl.ds(pl.multiple_of(part * LANES, LANES), LANES)
            there = pl.ds(pl.multiple_of(part * LANES + PAD * deep, SUB), LANES)
            turned = [field[c, there, :].T for c in range(4)]
            b_lo, c_lo = edge_lo[0, :, here], edge_lo[1, :, here]
            a_hi, c_hi = edge_hi[0, :, here], edge_hi[1, :, here]
            a_lo, b_hi = b_lo + 16.0 * c_lo, a_hi - 16.0 * c_hi
            e_lo = [value[:SUB, :] for value in turned]
            e_hi = [value[tile_y - SUB :, :] for value in turned]
            for c in range(4):
                flow_a, flow_c = a_lo * e_lo[c], c_lo * e_lo[c]
                flow_b, flow_d = b_hi * e_hi[c], c_hi * e_hi[c]
                if c < 2:
                    flow_a = flow_a + pressure[c] * third * e_lo[3]
                    flow_c = flow_c + pressure[c] * twelfth * e_lo[3]
                    flow_b = flow_b - pressure[c] * third * e_hi[3]
                    flow_d = flow_d + pressure[c] * twelfth * e_hi[3]
                y_send[turn, 0, 2 * c : 2 * c + 1, here] = -flow_c[0:1, :]
                y_send[turn, 0, 2 * c + 1 : 2 * c + 2, here] = flow_a[0:1, :] - flow_c[1:2, :]
                y_send[turn, 1, 2 * c : 2 * c + 1, here] = flow_b[7:8, :] + flow_d[6:7, :]
                y_send[turn, 1, 2 * c + 1 : 2 * c + 2, here] = flow_d[7:8, :]

        for side in range(2):
            copy = pltpu.make_async_remote_copy(
                src_ref=y_send.at[turn, side],
                dst_ref=y_recv.at[turn, side],
                send_sem=send_sem.at[turn, 2 + side],
                recv_sem=recv_sem.at[turn, 2 + side],
                device_id=peers[2 + side],
                device_id_type=MESH,
            )
            copy.start()
            copies.append(copy)

        @pl.loop(0, tile_x)
        def _(row):
            x = row + PAD
            centre_weight = jnp.broadcast_to(1.0 - 4.0 * kappa[pl.ds(x, 1), :], (SUB, tile_y))
            for t in range(deep // SUB):
                at = pl.ds(pl.multiple_of(row * deep, SUB) + t * SUB, SUB)
                here = pl.ds(pl.multiple_of(x * deep, SUB) + t * SUB, SUB)
                e = [field[c, here, :] for c in range(4)]
                a, b, m, p = north_a[at, :], north_b[at, :], north_m[at, :], north_p[at, :]
                push_a, push_b, push_m, push_p = wide_a * e[3], wide_b * e[3], wide_m * e[3], wide_p * e[3]
                flow_x = x_parts(x, t)
                for c in range(4):
                    flow_a, flow_b, flow_m, flow_p = a * e[c], b * e[c], m * e[c], p * e[c]
                    if c < 2:
                        flow_a = flow_a + pressure[c] * push_a
                        flow_b = flow_b - pressure[c] * push_b
                        flow_m = flow_m + pressure[c] * push_m
                        flow_p = flow_p + pressure[c] * push_p
                    down_y = pltpu.roll(flow_a, tile_y - 1, 1) - pltpu.roll(flow_m, tile_y - 2, 1)
                    up_y = pltpu.roll(flow_b, 1, 1) + pltpu.roll(flow_p, 2, 1)
                    total = (centre_weight * e[c] + flow_x[c]) + (down_y + up_y)
                    if c == 2:
                        total = total - cor * e[3]
                    if c == 3:
                        total = total + cor * e[2]
                    result[c, at, :] = total

        for copy in copies[2:]:
            copy.wait()

        from_north = (me_y < span_y - 1).astype(F32)
        from_south = (me_y > 0).astype(F32)

        @pl.loop(0, rows // LANES)
        def _(part):
            here = pl.ds(pl.multiple_of(part * LANES, LANES), LANES)
            place = lax.broadcasted_iota(jnp.int32, (SUB, LANES), 0)
            got_north = y_recv[turn, 0, :, here] * from_north
            got_south = y_recv[turn, 1, :, here] * from_south
            for c in range(4):
                low = jnp.where(
                    place == 0, got_south[2 * c : 2 * c + 1, :], jnp.where(place == 1, got_south[2 * c + 1 : 2 * c + 2, :], 0.0)
                )
                high = jnp.where(
                    place == SUB - 2, got_north[2 * c : 2 * c + 1, :],
                    jnp.where(place == SUB - 1, got_north[2 * c + 1 : 2 * c + 2, :], 0.0),
                )
                whole = jnp.concatenate([low, jnp.zeros((tile_y - 2 * SUB, LANES), F32), high], axis=0)
                result[c, here, :] = result[c, here, :] + whole.T

        for copy in copies[:2]:
            copy.wait()

        from_east = (me_x < span_x - 1).astype(F32)
        from_west = (me_x > 0).astype(F32)
        for side, factor in ((0, from_east), (1, from_west)):
            for place in range(2):
                row = (tile_x - 2 + place) if side == 0 else place
                for c in range(4):
                    at = slice(row * deep, (row + 1) * deep)
                    result[c, at, :] = result[c, at, :] + factor * x_recv[turn, side, place, c]

    @pl.loop(0, levels)
    def _(l):
        under = l < wet
        for c in range(4):
            out_ref[c, l] = jnp.where(under, result[c, pl.ds(l, tile_x, stride=deep), :], 0.0)


def on_device(
    adjoint_state, velocity, diffusivity, mixing, wet_levels, innovations, owner_tile, cell_index, offsets,
    live_counts, depth_weights,
):
    levels, tile_x, tile_y = adjoint_state.shape[1:]
    deep = -(-levels // SUB) * SUB
    span_x, span_y = lax.axis_size("gx"), lax.axis_size("gy")
    tiles = span_x * span_y
    obs = innovations.shape[0]
    prof = depth_weights.shape[0]
    rows = tile_x * deep
    wide = (tile_x + 2 * PAD) * deep
    hbm = pl.BlockSpec(memory_space=pltpu.HBM)
    vmem = lambda *shape: pltpu.VMEM(shape, F32)
    return pl.pallas_call(
        functools.partial(
            whole_kernel, levels=levels, deep=deep, span_x=span_x, span_y=span_y, total_rows=tile_y * span_y
        ),
        in_specs=[pl.BlockSpec(memory_space=pltpu.SMEM)] + [hbm] * 10,
        out_specs=pl.BlockSpec(memory_space=pltpu.VMEM),
        out_shape=jax.ShapeDtypeStruct(adjoint_state.shape, F32),
        scratch_shapes=[
            pltpu.VMEM((1, obs), jnp.int32),
            pltpu.VMEM((1, obs), jnp.int32),
            vmem(2, obs),
            vmem(obs, LANES),
            vmem(levels, prof),
            vmem(4, levels, tile_x, tile_y),
            vmem(2, levels, tile_x, tile_y),
            vmem(tile_x, tile_y),
            vmem(tile_x, tile_y),
            pltpu.VMEM((tile_x, tile_y), jnp.int32),
            pltpu.VMEM((obs, 2 * LANES), BF16),
            pltpu.VMEM((1, obs), jnp.int32),
            vmem(tiles, CAP, LANES),
            vmem(tiles, CAP, LANES),
            pltpu.VMEM((4 * deep, GROUP * CAP), BF16),
            vmem(SUB, GROUP * CAP),
            vmem(tile_y, GROUP * CAP),
            vmem(tile_x * 2 * deep, tile_y),
            vmem(4, wide, tile_y),
            vmem(wide, tile_y),
            vmem(wide, tile_y),
            vmem(wide, tile_y),
            vmem(rows, tile_y),
            vmem(rows, tile_y),
            vmem(rows, tile_y),
            vmem(rows, tile_y),
            vmem(tile_x + 2 * PAD, tile_y),
            vmem(4, rows, tile_y),
            vmem(levels, tile_x, tile_y),
            vmem(levels, tile_x, tile_y),
            vmem(4, levels, tile_x, tile_y),
            vmem(2, SUB, rows),
            vmem(2, SUB, rows),
            vmem(2, 2, 2, 4, deep, tile_y),
            vmem(2, 2, 2, 4, deep, tile_y),
            vmem(2, 2, SUB, rows),
            vmem(2, 2, SUB, rows),
            pltpu.SemaphoreType.DMA((10,)),
            pltpu.SemaphoreType.DMA,
            pltpu.SemaphoreType.DMA((tiles // GROUP,)),
            pltpu.SemaphoreType.DMA((2, 4)),
            pltpu.SemaphoreType.DMA((2, 4)),
        ],
        compiler_params=pltpu.CompilerParams(collective_id=0, has_side_effects=True, vmem_limit_bytes=60 << 20),
        name="whole",
    )(
        live_counts, owner_tile.reshape(1, obs), cell_index.reshape(1, obs), offsets, innovations, depth_weights.T,
        adjoint_state, velocity, diffusivity, mixing, wet_levels,
    )


def solution(mesh):
    placed = (
        P(None, None, "gx", "gy"),
        P(None, None, "gx", "gy"),
        P("gx", "gy"),
        P("gx", "gy"),
        P("gx", "gy"),
        P(("gx", "gy"), None),
        P(("gx", "gy"), None),
        P(("gx", "gy")),
        P(None, ("gx", "gy")),
        P(("gx", "gy")),
        P(),
    )
    return jax.shard_map(
        on_device, mesh=mesh, in_specs=placed, out_specs=P(None, None, "gx", "gy"), check_vma=False
    )
```

```python
import functools

import jax
import jax.numpy as jnp
from jax import lax
from jax.experimental import pallas as pl
from jax.experimental.pallas import tpu as pltpu
from jax.sharding import PartitionSpec as P

F32 = jnp.float32
BF16 = jnp.bfloat16
MESH = pl.DeviceIdType.MESH

PRESSURE_HEAT = 0.2
PRESSURE_SALT = 0.15
CORIOLIS_PEAK = 0.2

CAP = 24
LANES = 128
SUB = 8
PAD = 4


def split(value):
    high = value.astype(BF16)
    return high, (value - high.astype(F32)).astype(BF16)


GROUP = 32
BURST = 8
AHEAD = 6


def whole_kernel(
    live_ref, target_hbm, cell_hbm, offset_hbm, rows_hbm, weights_hbm, state_hbm, velocity_hbm, diffusion_hbm,
    mixing_hbm, wet_hbm, out_ref,
    target_ref, cell_ref, offset_ref, rows_ref, weights_ref, state_ref, velocity_ref, diffusion_ref, mixing_ref,
    wet_ref, packed, slots, send, recv, values, sides, columns,
    field, east_a, east_b, east_c, north_a, north_b, north_m, north_p, kappa, result, inverse, gain, going,
    edge_lo, edge_hi, x_send, x_recv, y_send, y_recv,
    local_sem, row_send_sem, row_recv_sem, send_sem, recv_sem,
    *, levels, deep, span_x, span_y, total_rows,
):
    tile_x, tile_y = mixing_ref.shape
    rows = tile_x * deep
    tiles = span_x * span_y
    obs = rows_ref.shape[0]
    prof = weights_ref.shape[1]
    me_x, me_y = lax.axis_index("gx"), lax.axis_index("gy")
    west, right = lax.rem(me_x + span_x - 1, span_x), lax.rem(me_x + 1, span_x)
    south, up = lax.rem(me_y + span_y - 1, span_y), lax.rem(me_y + 1, span_y)
    peers = ((west, me_y), (right, me_y), (me_x, south), (me_x, up))

    moves = [
        pltpu.make_async_copy(source, target, local_sem.at[place])
        for place, (source, target) in enumerate(
            (
                (target_hbm, target_ref), (cell_hbm, cell_ref), (offset_hbm, offset_ref), (weights_hbm, weights_ref),
                (rows_hbm, rows_ref), (mixing_hbm, mixing_ref), (diffusion_hbm, diffusion_ref), (wet_hbm, wet_ref),
                (velocity_hbm, velocity_ref), (state_hbm, state_ref),
            )
        )
    ]
    for move in moves:
        move.start()

    others = [
        (lax.rem(me_x + t % span_x, span_x), lax.rem(me_y + t // span_x + 2 * (t % span_x), span_y))
        for t in range(1, tiles)
    ]
    barrier = pltpu.get_barrier_semaphore()
    for other in others:
        pl.semaphore_signal(barrier, inc=1, device_id=other, device_id_type=MESH)

    for move in moves[:5]:
        move.wait()

    wide = jnp.concatenate([weights_ref[...], jnp.zeros((levels, LANES - prof), F32)], axis=1)
    gap = jnp.zeros((deep - levels, LANES), F32)
    both = jnp.concatenate(
        [wide, gap, pltpu.roll(wide, prof, 1), gap, jnp.zeros((LANES - 2 * deep, LANES), F32)], axis=0
    ).T
    tri = (
        lax.broadcasted_iota(jnp.int32, (256, 256), 0) < lax.broadcasted_iota(jnp.int32, (256, 256), 1)
    ).astype(BF16)
    tile_place = lax.broadcasted_iota(jnp.int32, (tiles, 256), 0)
    carry = jnp.zeros((tiles, 1), F32)
    for part in range(obs // 256):
        span = slice(part * 256, (part + 1) * 256)
        place = lax.broadcasted_iota(jnp.int32, (1, 256), 1) + part * 256
        live = place < live_ref[0]
        target = target_ref[:, span]
        named = ((tile_place == target) & live).astype(F32)
        before = jnp.dot(named.astype(BF16), tri, preferred_element_type=F32) + carry
        rank = jnp.sum(named * before, axis=0, keepdims=True)
        carry = carry + jnp.sum(named, axis=1, keepdims=True)
        slots[:, span] = jnp.where(live, target * CAP + rank.astype(jnp.int32), -1)
        cell = cell_ref[:, span].astype(F32)
        cell_row = jnp.floor((cell + 0.5) * (1.0 / (tile_y - 1)))
        cell_col = cell - (tile_y - 1.0) * cell_row
        for half in range(2):
            cut = slice(half * LANES, (half + 1) * LANES)
            here = slice(part * 256 + half * LANES, part * 256 + (half + 1) * LANES)
            side = jnp.concatenate(
                [
                    jnp.zeros((2 * deep, LANES), F32), cell_row[:, cut], cell_col[:, cut], offset_ref[:, here],
                    jnp.zeros((LANES - 2 * deep - 4, LANES), F32),
                ],
                axis=0,
            )
            profile = jnp.dot(rows_ref[here, :], both, precision=lax.Precision.HIGHEST, preferred_element_type=F32)
            high, low = split(profile + side.T)
            packed[here, :LANES] = high
            packed[here, LANES:] = low

    def send_burst(burst):
        for t in range(burst * BURST, min((burst + 1) * BURST, len(others))):
            pltpu.make_async_remote_copy(
                src_ref=send.at[t], dst_ref=recv.at[t], send_sem=row_send_sem, recv_sem=row_recv_sem.at[t // GROUP],
                device_id=others[t], device_id_type=MESH,
            ).start()

    named_tiles = others + [(me_x, me_y)]
    for burst in range(tiles // BURST):
        cut = slice(burst * BURST, (burst + 1) * BURST)
        slot = lax.broadcasted_iota(jnp.int32, (CAP, 1), 0)
        place = jnp.concatenate([slot + (x * span_y + y) * CAP for x, y in named_tiles[cut]], axis=0)
        pick = (place == slots[...]).astype(F32).astype(BF16)
        got = jnp.dot(pick, packed[...], preferred_element_type=F32)
        got = got[:, :LANES] + got[:, LANES:]
        send[cut] = got.reshape(BURST, CAP, LANES)
        if burst == AHEAD - 1:
            pl.semaphore_wait(barrier, len(others))
            for early in range(AHEAD):
                send_burst(early)
        if burst >= AHEAD:
            send_burst(burst)
    recv[tiles - 1] = send[tiles - 1]

    for move in moves[5:]:
        move.wait()
    mixing = mixing_ref[...]
    lane = lax.broadcasted_iota(jnp.int32, (1, tile_y), 1)
    third, twelfth = 8.0 / 12.0, 1.0 / 12.0

    def coefficient(l, q_before):
        diag = 1.0 + mixing * jnp.where((l == 0) | (l == levels - 1), 1.0, 2.0)
        q = 1.0 / (diag - mixing * mixing * q_before)
        inverse[l] = q
        gain[l] = mixing * q
        return q

    lax.fori_loop(0, levels, coefficient, jnp.zeros_like(mixing))

    zero_rows = jnp.zeros((PAD * deep, tile_y), F32)
    for c in range(4):
        field[c, : PAD * deep, :] = zero_rows
        field[c, (PAD + tile_x) * deep :, :] = zero_rows
    for table in (east_a, east_b, east_c):
        table[: PAD * deep, :] = zero_rows
        table[(PAD + tile_x) * deep :, :] = zero_rows
    kappa[...] = jnp.zeros_like(kappa)
    kappa[PAD : PAD + tile_x, :] = diffusion_ref[...]

    @pl.loop(0, deep - levels)
    def _(extra):
        blank = jnp.zeros((tile_x, tile_y), F32)
        for c in range(4):
            field[c, pl.ds(PAD * deep + levels + extra, tile_x, stride=deep), :] = blank
            result[c, pl.ds(levels + extra, tile_x, stride=deep), :] = blank
        for table in (east_a, east_b, east_c):
            table[pl.ds(PAD * deep + levels + extra, tile_x, stride=deep), :] = blank
        for table in (north_a, north_b, north_m, north_p):
            table[pl.ds(levels + extra, tile_x, stride=deep), :] = blank

    diffusion = diffusion_ref[...]
    mask_a = (lane >= 1).astype(F32)
    mask_b = (lane < tile_y - 1).astype(F32)
    mask_m = (lane >= 2).astype(F32)
    mask_p = (lane < tile_y - 2).astype(F32)

    @pl.loop(0, levels)
    def _(l):
        for c in range(4):
            result[c, pl.ds(l, tile_x, stride=deep), :] = state_ref[c, l]
        u, v = velocity_ref[0, l], velocity_ref[1, l]
        there = pl.ds(PAD * deep + l, tile_x, stride=deep)
        east_a[there, :] = third * u + diffusion
        east_b[there, :] = diffusion - third * u
        east_c[there, :] = twelfth * u
        here = pl.ds(l, tile_x, stride=deep)
        north_a[here, :] = (third * v + diffusion) * mask_a
        north_b[here, :] = (diffusion - third * v) * mask_b
        north_m[here, :] = (twelfth * v) * mask_m
        north_p[here, :] = (twelfth * v) * mask_p

    @pl.loop(0, rows // LANES)
    def _(part):
        here = pl.ds(pl.multiple_of(part * LANES, LANES), LANES)
        edge_lo[0, :, here] = north_b[here, :].T[:SUB, :]
        edge_lo[1, :, here] = north_p[here, :].T[:SUB, :]
        edge_hi[0, :, here] = north_a[here, :].T[tile_y - SUB :, :]
        edge_hi[1, :, here] = north_m[here, :].T[tile_y - SUB :, :]

    cor = CORIOLIS_PEAK * (2.0 * ((lane + me_y * tile_y).astype(F32) + 0.5) / total_rows - 1.0)
    full = (SUB, tile_y)
    cor = jnp.broadcast_to(cor, full)
    wide_a, wide_b = jnp.broadcast_to(third * mask_a, full), jnp.broadcast_to(third * mask_b, full)
    wide_m, wide_p = jnp.broadcast_to(twelfth * mask_m, full), jnp.broadcast_to(twelfth * mask_p, full)
    wet = wet_ref[...]
    pressure = (PRESSURE_HEAT, -PRESSURE_SALT)

    def x_parts(x, t):
        def at(shift):
            return pl.ds(pl.multiple_of((x + shift) * deep, SUB) + t * SUB, SUB)

        up_1, down_1, up_2, down_2 = at(1), at(-1), at(2), at(-2)
        a, b, c_up, c_down = east_a[up_1, :], east_b[down_1, :], east_c[up_2, :], east_c[down_2, :]
        totals = []
        for c in range(4):
            e_up, e_down, e_up_2, e_down_2 = (field[c, place, :] for place in (up_1, down_1, up_2, down_2))
            totals.append((a * e_up + b * e_down) + (c_down * e_down_2 - c_up * e_up_2))
            if c == 2:
                push = third * (e_up - e_down) - twelfth * (e_up_2 - e_down_2)
        return [totals[0] + pressure[0] * push, totals[1] + pressure[1] * push, totals[2], totals[3]]

    count = GROUP * CAP
    y_place = lax.broadcasted_iota(jnp.int32, (tile_y, LANES), 0).astype(F32)
    for group in range(tiles // GROUP):
        came = pl.ds(group * GROUP, min(GROUP, len(others) - group * GROUP))
        pltpu.make_async_remote_copy(
            src_ref=send.at[came], dst_ref=recv.at[came], send_sem=row_send_sem, recv_sem=row_recv_sem.at[group],
            device_id=peers[0], device_id_type=MESH,
        ).wait_recv()
        table = recv[group * GROUP : (group + 1) * GROUP].reshape(count, LANES)
        for part in range(count // LANES):
            here = slice(part * LANES, (part + 1) * LANES)
            turned = table[here].T
            high, low = split(turned[: 2 * deep])
            values[: 2 * deep, here] = high
            values[2 * deep :, here] = low
            side = turned[2 * deep : 2 * deep + SUB]
            sides[:, here] = side
            col, north = side[1:2, :], side[3:4, :]
            columns[:, here] = jnp.where(y_place == col, 1.0 - north, 0.0) + jnp.where(y_place == col + 1.0, north, 0.0)

        @pl.loop(0, tile_x // 2)
        def _(pair):
            cell_row, aside = sides[0:1, :], sides[2:3, :]
            high, low = [], []
            for half in range(2):
                x_now = (2 * pair + half).astype(F32)
                share = jnp.where(cell_row == x_now, 1.0 - aside, 0.0) + jnp.where(cell_row + 1.0 == x_now, aside, 0.0)
                one, two = split(columns[...] * share)
                high.append(one)
                low.append(two)
            across = (((1,), (1,)), ((), ()))
            got = lax.dot_general(values[...], jnp.concatenate(high, axis=0), across, preferred_element_type=F32)
            rest = lax.dot_general(
                values[: 2 * deep], jnp.concatenate(low, axis=0), across, preferred_element_type=F32
            )
            total = got[: 2 * deep] + got[2 * deep :] + rest
            for half in range(2):
                at = pl.ds(pl.multiple_of((2 * pair + half) * deep, SUB), deep)
                for c in range(2):
                    part = total[c * deep : (c + 1) * deep, half * tile_y : (half + 1) * tile_y]
                    result[c, at, :] = result[c, at, :] + part

    sent = pl.ds(0, len(others))
    pltpu.make_async_remote_copy(
        src_ref=send.at[sent], dst_ref=recv.at[sent], send_sem=row_send_sem, recv_sem=row_recv_sem.at[0],
        device_id=peers[0], device_id_type=MESH,
    ).wait_send()

    def fives(body):
        def run(k, carry):
            for one in range(5):
                carry = body(5 * k + one, carry)
            return carry

        return run

    @pl.loop(0, 2)
    def _(turn):
        def down(l, before):
            now = []
            q, p = inverse[l], gain[l]
            under = l < wet
            for c in range(4):
                value = result[c, pl.ds(l, tile_x, stride=deep), :]
                value = jnp.where(under, value, 0.0) * q + p * before[c]
                going[c, l] = value
                now.append(value)
            return tuple(now)

        lax.fori_loop(0, levels // 5, fives(down), (jnp.zeros((tile_x, tile_y), F32),) * 4)

        def rise(k, below):
            l = levels - 1 - k
            p = jnp.where(k == 0, 0.0, 1.0) * gain[l]
            now = []
            for c in range(4):
                value = going[c, l] + p * below[c]
                field[c, pl.ds(PAD * deep + l, tile_x, stride=deep), :] = value
                now.append(value)
            return tuple(now)

        lax.fori_loop(0, levels // 5, fives(rise), (jnp.zeros((tile_x, tile_y), F32),) * 4)

        copies = []
        for side in range(2):
            for place in range(2):
                x = (PAD - 2 + place) if side == 0 else (PAD + tile_x + place)
                for t in range(deep // SUB):
                    for c, part in enumerate(x_parts(x, t)):
                        x_send[turn, side, place, c, t * SUB : (t + 1) * SUB, :] = part
            copy = pltpu.make_async_remote_copy(
                src_ref=x_send.at[turn, side, :, :, pl.ds(0, levels)],
                dst_ref=x_recv.at[turn, side, :, :, pl.ds(0, levels)],
                send_sem=send_sem.at[turn, side],
                recv_sem=recv_sem.at[turn, side],
                device_id=peers[side],
                device_id_type=MESH,
            )
            copy.start()
            copies.append(copy)

        @pl.loop(0, rows // LANES)
        def _(part):
            here = pl.ds(pl.multiple_of(part * LANES, LANES), LANES)
            there = pl.ds(pl.multiple_of(part * LANES + PAD * deep, SUB), LANES)
            turned = [field[c, there, :].T for c in range(4)]
            b_lo, c_lo = edge_lo[0, :, here], edge_lo[1, :, here]
            a_hi, c_hi = edge_hi[0, :, here], edge_hi[1, :, here]
            a_lo, b_hi = b_lo + 16.0 * c_lo, a_hi - 16.0 * c_hi
            e_lo = [value[:SUB, :] for value in turned]
            e_hi = [value[tile_y - SUB :, :] for value in turned]
            for c in range(4):
                flow_a, flow_c = a_lo * e_lo[c], c_lo * e_lo[c]
                flow_b, flow_d = b_hi * e_hi[c], c_hi * e_hi[c]
                if c < 2:
                    flow_a = flow_a + pressure[c] * third * e_lo[3]
                    flow_c = flow_c + pressure[c] * twelfth * e_lo[3]
                    flow_b = flow_b - pressure[c] * third * e_hi[3]
                    flow_d = flow_d + pressure[c] * twelfth * e_hi[3]
                y_send[turn, 0, 2 * c : 2 * c + 1, here] = -flow_c[0:1, :]
                y_send[turn, 0, 2 * c + 1 : 2 * c + 2, here] = flow_a[0:1, :] - flow_c[1:2, :]
                y_send[turn, 1, 2 * c : 2 * c + 1, here] = flow_b[7:8, :] + flow_d[6:7, :]
                y_send[turn, 1, 2 * c + 1 : 2 * c + 2, here] = flow_d[7:8, :]

        for side in range(2):
            copy = pltpu.make_async_remote_copy(
                src_ref=y_send.at[turn, side],
                dst_ref=y_recv.at[turn, side],
                send_sem=send_sem.at[turn, 2 + side],
                recv_sem=recv_sem.at[turn, 2 + side],
                device_id=peers[2 + side],
                device_id_type=MESH,
            )
            copy.start()
            copies.append(copy)

        @pl.loop(0, tile_x)
        def _(row):
            x = row + PAD
            centre_weight = jnp.broadcast_to(1.0 - 4.0 * kappa[pl.ds(x, 1), :], (SUB, tile_y))
            for t in range(deep // SUB):
                at = pl.ds(pl.multiple_of(row * deep, SUB) + t * SUB, SUB)
                here = pl.ds(pl.multiple_of(x * deep, SUB) + t * SUB, SUB)
                e = [field[c, here, :] for c in range(4)]
                a, b, m, p = north_a[at, :], north_b[at, :], north_m[at, :], north_p[at, :]
                push_a, push_b, push_m, push_p = wide_a * e[3], wide_b * e[3], wide_m * e[3], wide_p * e[3]
                flow_x = x_parts(x, t)
                for c in range(4):
                    flow_a, flow_b, flow_m, flow_p = a * e[c], b * e[c], m * e[c], p * e[c]
                    if c < 2:
                        flow_a = flow_a + pressure[c] * push_a
                        flow_b = flow_b - pressure[c] * push_b
                        flow_m = flow_m + pressure[c] * push_m
                        flow_p = flow_p + pressure[c] * push_p
                    down_y = pltpu.roll(flow_a, tile_y - 1, 1) - pltpu.roll(flow_m, tile_y - 2, 1)
                    up_y = pltpu.roll(flow_b, 1, 1) + pltpu.roll(flow_p, 2, 1)
                    total = (centre_weight * e[c] + flow_x[c]) + (down_y + up_y)
                    if c == 2:
                        total = total - cor * e[3]
                    if c == 3:
                        total = total + cor * e[2]
                    result[c, at, :] = total

        for copy in copies[2:]:
            copy.wait()

        from_north = (me_y < span_y - 1).astype(F32)
        from_south = (me_y > 0).astype(F32)

        @pl.loop(0, rows // LANES)
        def _(part):
            here = pl.ds(pl.multiple_of(part * LANES, LANES), LANES)
            place = lax.broadcasted_iota(jnp.int32, (SUB, LANES), 0)
            got_north = y_recv[turn, 0, :, here] * from_north
            got_south = y_recv[turn, 1, :, here] * from_south
            for c in range(4):
                low = jnp.where(
                    place == 0, got_south[2 * c : 2 * c + 1, :], jnp.where(place == 1, got_south[2 * c + 1 : 2 * c + 2, :], 0.0)
                )
                high = jnp.where(
                    place == SUB - 2, got_north[2 * c : 2 * c + 1, :],
                    jnp.where(place == SUB - 1, got_north[2 * c + 1 : 2 * c + 2, :], 0.0),
                )
                whole = jnp.concatenate([low, jnp.zeros((tile_y - 2 * SUB, LANES), F32), high], axis=0)
                result[c, here, :] = result[c, here, :] + whole.T

        for copy in copies[:2]:
            copy.wait()

        from_east = (me_x < span_x - 1).astype(F32)
        from_west = (me_x > 0).astype(F32)
        for side, factor in ((0, from_east), (1, from_west)):
            for place in range(2):
                row = (tile_x - 2 + place) if side == 0 else place
                for c in range(4):
                    at = slice(row * deep, row * deep + levels)
                    result[c, at, :] = result[c, at, :] + factor * x_recv[turn, side, place, c, :levels]

    @pl.loop(0, levels)
    def _(l):
        under = l < wet
        for c in range(4):
            out_ref[c, l] = jnp.where(under, result[c, pl.ds(l, tile_x, stride=deep), :], 0.0)


def on_device(
    adjoint_state, velocity, diffusivity, mixing, wet_levels, innovations, owner_tile, cell_index, offsets,
    live_counts, depth_weights,
):
    levels, tile_x, tile_y = adjoint_state.shape[1:]
    deep = -(-levels // SUB) * SUB
    span_x, span_y = lax.axis_size("gx"), lax.axis_size("gy")
    tiles = span_x * span_y
    obs = innovations.shape[0]
    prof = depth_weights.shape[0]
    rows = tile_x * deep
    wide = (tile_x + 2 * PAD) * deep
    hbm = pl.BlockSpec(memory_space=pltpu.HBM)
    vmem = lambda *shape: pltpu.VMEM(shape, F32)
    return pl.pallas_call(
        functools.partial(
            whole_kernel, levels=levels, deep=deep, span_x=span_x, span_y=span_y, total_rows=tile_y * span_y
        ),
        in_specs=[pl.BlockSpec(memory_space=pltpu.SMEM)] + [hbm] * 10,
        out_specs=pl.BlockSpec(memory_space=pltpu.VMEM),
        out_shape=jax.ShapeDtypeStruct(adjoint_state.shape, F32),
        scratch_shapes=[
            pltpu.VMEM((1, obs), jnp.int32),
            pltpu.VMEM((1, obs), jnp.int32),
            vmem(2, obs),
            vmem(obs, LANES),
            vmem(levels, prof),
            vmem(4, levels, tile_x, tile_y),
            vmem(2, levels, tile_x, tile_y),
            vmem(tile_x, tile_y),
            vmem(tile_x, tile_y),
            pltpu.VMEM((tile_x, tile_y), jnp.int32),
            pltpu.VMEM((obs, 2 * LANES), BF16),
            pltpu.VMEM((1, obs), jnp.int32),
            vmem(tiles, CAP, LANES),
            vmem(tiles, CAP, LANES),
            pltpu.VMEM((4 * deep, GROUP * CAP), BF16),
            vmem(SUB, GROUP * CAP),
            vmem(tile_y, GROUP * CAP),
            vmem(4, wide, tile_y),
            vmem(wide, tile_y),
            vmem(wide, tile_y),
            vmem(wide, tile_y),
            vmem(rows, tile_y),
            vmem(rows, tile_y),
            vmem(rows, tile_y),
            vmem(rows, tile_y),
            vmem(tile_x + 2 * PAD, tile_y),
            vmem(4, rows, tile_y),
            vmem(levels, tile_x, tile_y),
            vmem(levels, tile_x, tile_y),
            vmem(4, levels, tile_x, tile_y),
            vmem(2, SUB, rows),
            vmem(2, SUB, rows),
            vmem(2, 2, 2, 4, deep, tile_y),
            vmem(2, 2, 2, 4, deep, tile_y),
            vmem(2, 2, SUB, rows),
            vmem(2, 2, SUB, rows),
            pltpu.SemaphoreType.DMA((10,)),
            pltpu.SemaphoreType.DMA,
            pltpu.SemaphoreType.DMA((tiles // GROUP,)),
            pltpu.SemaphoreType.DMA((2, 4)),
            pltpu.SemaphoreType.DMA((2, 4)),
        ],
        compiler_params=pltpu.CompilerParams(collective_id=0, has_side_effects=True, vmem_limit_bytes=60 << 20),
        name="whole",
    )(
        live_counts, owner_tile.reshape(1, obs), cell_index.reshape(1, obs), offsets, innovations, depth_weights.T,
        adjoint_state, velocity, diffusivity, mixing, wet_levels,
    )


def solution(mesh):
    placed = (
        P(None, None, "gx", "gy"),
        P(None, None, "gx", "gy"),
        P("gx", "gy"),
        P("gx", "gy"),
        P("gx", "gy"),
        P(("gx", "gy"), None),
        P(("gx", "gy"), None),
        P(("gx", "gy")),
        P(None, ("gx", "gy")),
        P(("gx", "gy")),
        P(),
    )
    return jax.shard_map(
        on_device, mesh=mesh, in_specs=placed, out_specs=P(None, None, "gx", "gy"), check_vma=False
    )
```
